32 devices in a mesh: wide: 8 (over z, x), narrow: 4 (over y, core).
Axes of the slice: x: 2, y: 2, z: 4, core: 2. Of those that a mesh axis runs over, the one named last changes fastest.
Arguments:
- points: bfloat16 [32768, 256], P('wide'), may hold values from -6 to 6
- q_init: float32 [16, 32768], P(None, 'wide'), may hold values from -80 to 80
- pairs: int32 [2, 2048], P(None, ('wide', 'narrow')), may hold values from 0 to 255, as said below
Outputs:
- basis: float32 [16, 32768], P(None, 'wide')
- coeffs: float32 [3, 2, 16, 16], replicated
The draws below stay inside these ranges and needn't reach their ends.
Inputs may be any that keep to these rules, and one draw needn't show every extreme that they name: `pairs`: pair number g * 4 * 64 + m * 64 + o * 8 + c (g < 8, m < 4, o < 8, c < 8) has its first block in g * 32 .. (g + 1) * 32 - 1 and its second block in o * 32 .. (o + 1) * 32 - 1; the two ends of a pair differ.
All inputs are finite; a program needn't handle non-finite values.
Results may differ from the reference program's by a relative error of at most 0.0015.
Values may be sent and summed in bfloat16 or wider, within the bound.
A program may use at most 64 MiB of HBM per device.

```python
import jax
import jax.numpy as jnp
from jax import lax

F = 256
R = 16
BS = 128
STEPS = 3
PAIRS_DEV = 64
BLOCKS_PER_SHARD = 32
CAP = 8
NB = 256
NPTS = 32768
TOTAL_PAIRS = 2048
N_NARROW = 4


def draw_pairs(key, part):
    slot = jnp.arange(TOTAL_PAIRS, dtype=jnp.int32)
    device = slot // PAIRS_DEV
    group = device // N_NARROW
    owner = slot % PAIRS_DEV // CAP
    first_row = jax.random.randint(jax.random.fold_in(key, 11), (TOTAL_PAIRS,), 0, BLOCKS_PER_SHARD, dtype=jnp.int32)
    offset = jax.random.randint(jax.random.fold_in(key, 12), (TOTAL_PAIRS,), 1, BLOCKS_PER_SHARD, dtype=jnp.int32)
    other = jax.random.randint(jax.random.fold_in(key, 13), (TOTAL_PAIRS,), 0, BLOCKS_PER_SHARD, dtype=jnp.int32)
    second_row = jnp.where(owner == group, (first_row + offset) % BLOCKS_PER_SHARD, other)
    first_id = group * BLOCKS_PER_SHARD + first_row
    second_id = owner * BLOCKS_PER_SHARD + second_row
    return jnp.stack([first_id, second_id]).astype(jnp.int32)


def draw_q_init(key, part):
    noise = jax.random.normal(jax.random.fold_in(key, 21), (R, NPTS), jnp.float32)
    noise = jnp.clip(noise, -6.0, 6.0)
    scales = jnp.exp(jax.random.uniform(jax.random.fold_in(key, 22), (1, NPTS), jnp.float32, 0.0, 2.3))
    values = scales * noise
    return jnp.clip(values, -80.0, 80.0).astype(jnp.float32)


def level_of(stream_key, extent, cuts, low, largest):
    loudness = 1.0
    for position, shards_of in cuts:
        steps = jax.random.uniform(jax.random.fold_in(jax.random.fold_in(stream_key, 6), position), (shards_of,), jnp.float32, low / len(cuts), largest / len(cuts))
        loudness = loudness * jnp.repeat(jnp.exp(steps), extent[position] // shards_of).reshape((-1,) + (1,) * (len(extent) - 1 - position))
    return loudness


def centred(rng, extent, deviation, limit, cuts=(), kind=jnp.bfloat16):
    entries = deviation * jax.random.normal(rng, extent, jnp.float32)
    if cuts:
        entries = entries * level_of(rng, extent, cuts, -0.22, 0.18)
    return jnp.clip(entries, -limit, limit).astype(kind)


def setup_inputs(seed: int = 0) -> dict:
    keys = jax.random.split(jax.random.key(seed), 4)
    points = centred(keys[0], (NPTS, F), 1.0, 6.0, ((0, 8),))
    q_init = draw_q_init(jax.random.fold_in(keys[3], 71), 0)
    pairs = draw_pairs(jax.random.fold_in(keys[3], 71), 0)
    return {"points": points, "q_init": q_init, "pairs": pairs}


KERNEL_FACTOR = 3.0
EPSILON = 1e-06
HIGH = lax.Precision.HIGHEST

def unit_rows(points):
    wide32 = points.astype(jnp.float32)
    scaled = wide32 * lax.rsqrt(lax.optimization_barrier(jnp.sum(wide32 * wide32, axis=-1, keepdims=True)) + EPSILON)
    return scaled.astype(jnp.bfloat16)

def apply_kernel(unit, vectors, pairs):
    rows = vectors.reshape(R, NB, BS).transpose(1, 0, 2)
    point_groups = pairs.reshape(2, TOTAL_PAIRS // PAIRS_DEV, PAIRS_DEV).transpose(1, 0, 2)

    def single_group(total, ends):
        first = ends[0]
        second = ends[1]
        inner_products = jnp.einsum('paf,pbf->pab', unit[first].astype(jnp.float32), unit[second].astype(jnp.float32), precision=HIGH)
        kernel_values = jnp.exp(KERNEL_FACTOR * (inner_products - 1.0))
        to_first = jnp.einsum('pab,prb->pra', kernel_values, rows[second], precision=HIGH)
        to_second = jnp.einsum('pab,pra->prb', kernel_values, rows[first], precision=HIGH)
        return (total.at[first].add(to_first).at[second].add(to_second), None)
    total = lax.scan(single_group, jnp.zeros_like(rows), point_groups)[0]
    return total.transpose(1, 0, 2).reshape(R, NPTS)

def reference(points, q_init, pairs):
    unit = unit_rows(points).reshape(NB, BS, F)
    gram0 = jnp.dot(q_init, q_init.T, precision=HIGH) / NPTS
    factor0 = jnp.linalg.cholesky(gram0)
    current = lax.linalg.triangular_solve(factor0, q_init, left_side=True, lower=True)
    previous = jnp.zeros_like(current)
    last = jnp.zeros((R, R), jnp.float32).astype(current.dtype)
    records = []
    for step in range(STEPS):
        image = apply_kernel(unit, current, pairs)
        residual = image - jnp.dot(last.T, previous, precision=HIGH)
        along = jnp.dot(current, residual.T, precision=HIGH) / NPTS
        remainder = residual - jnp.dot(along.T, current, precision=HIGH)
        gram = jnp.dot(remainder, remainder.T, precision=HIGH) / NPTS
        factor = jnp.linalg.cholesky(gram)
        records.append(jnp.stack([along, factor]))
        previous = current
        last = factor
        current = lax.linalg.triangular_solve(factor, remainder, left_side=True, lower=True)
    return (current, jnp.stack(records))
```

```python
import functools

import jax
import jax.numpy as jnp
from jax import lax
from jax.experimental import pallas as pl
from jax.experimental.pallas import tpu as pltpu
from jax.sharding import PartitionSpec as P

BS = 128
STEPS = 3
LEVELS = 32767.0
KERNEL_FACTOR = 3.0
EPSILON = 1e-06
LOG_STEPS = 256.0
HIGH = lax.Precision.HIGHEST
MESH = pl.DeviceIdType.MESH


def unit_rows(points):
    wide32 = points.astype(jnp.float32)
    scaled = wide32 * lax.rsqrt(jnp.sum(wide32 * wide32, axis=-1, keepdims=True) + EPSILON)
    return scaled.astype(jnp.bfloat16)


def split(x):
    high = x.astype(jnp.bfloat16)
    return high, (x - high.astype(jnp.float32)).astype(jnp.bfloat16)


def coded(x, axes=1):
    top = jnp.maximum(jnp.max(jnp.abs(x), axis=axes, keepdims=True), 1e-30)
    scaled = jnp.clip(jnp.round(x * (LEVELS / top)), -LEVELS, LEVELS)
    return scaled.astype(jnp.int32).astype(jnp.int16), top * (1.0 / LEVELS)


def number(x):
    return x.astype(jnp.int32).astype(jnp.float32)


def dot32(a, b):
    return jnp.dot(a, b, precision=HIGH, preferred_element_type=jnp.float32)


def dot_nt(a, b, precision=None):
    return lax.dot_general(
        a, b, (((1,), (1,)), ((), ())), precision=precision, preferred_element_type=jnp.float32
    )


def tiles_kernel(capacity, me_ref, first_ref, unit_ref, second_ref, out_ref):
    d = pl.program_id(0)
    for c in range(capacity):
        s = dot_nt(unit_ref[first_ref[d * capacity + c]], second_ref[0, c])
        high, low = split(jnp.exp(KERNEL_FACTOR * (s - 1.0)))
        out_ref[c, :, :BS] = high
        out_ref[c, :, BS:] = low


def make_tiles(me, first, unit, second):
    wide_count, capacity, _, width = second.shape
    own_blocks = unit.shape[0]
    spec = pltpu.PrefetchScalarGridSpec(
        num_scalar_prefetch=2,
        grid=(wide_count,),
        in_specs=[
            pl.BlockSpec((own_blocks, BS, width), lambda d, m, f: (0, 0, 0)),
            pl.BlockSpec(
                (1, capacity, BS, width),
                lambda d, m, f: (lax.rem(m[0] - d + wide_count, wide_count), 0, 0, 0),
            ),
        ],
        out_specs=pl.BlockSpec((capacity, BS, 2 * BS), lambda d, m, f: (d, 0, 0)),
    )
    return pl.pallas_call(
        functools.partial(tiles_kernel, capacity),
        grid_spec=spec,
        out_shape=jax.ShapeDtypeStruct((wide_count * capacity, BS, 2 * BS), jnp.bfloat16),
        name="tiles",
    )(me, first, unit, second)


def factor_of(gram, r):
    i = lax.broadcasted_iota(jnp.int32, (r, r), 0)
    j = lax.broadcasted_iota(jnp.int32, (r, r), 1)
    both_i = lax.broadcasted_iota(jnp.int32, (r, 2 * r), 0)
    m = jnp.concatenate([gram, (i == j).astype(jnp.float32)], axis=1)
    lower = jnp.zeros((r, r), jnp.float32)
    for k in range(r):
        inv = 1.0 / jnp.sqrt(m[k : k + 1, k : k + 1])
        row = m[k : k + 1, :] * inv
        col = m[:, k : k + 1] * inv
        lower = jnp.where((j == k) & (i >= k), col, lower)
        m = jnp.where(both_i == k, row, jnp.where(both_i > k, m - col * row, m))
    upper = jnp.where(j >= i, m[:, :r], 0.0)
    inverse = jnp.where(j <= i, m[:, r:], 0.0)
    return lower, upper, inverse


def main_kernel(
    dims, first, local, owners, tiles, q_ref, out, coef,
    sb, rb, sb2, rq, ss, rs1, ss2, rs2, coded_blocks, scales, rb2, tf, pb, rs, ag, acc, out16, all16, psc, rsc, osc, asc, xs, blocks, prev, up, gs, gr,
    s1, r1, s2, r2, s3, r3, s4, r4, s5, r5, s6, r6, s7, r7, s8, r8, s9, r9,
):
    W, N, C, R, B, total = dims
    CR = C * R
    RN = R // N
    PR = RN * B
    me = lax.axis_index("wide")
    nar = lax.axis_index("narrow")

    def up_peer(d):
        return lax.rem(me + d, W)

    def down_peer(d):
        return lax.rem(me - d + W, W)

    barrier = pltpu.get_barrier_semaphore()
    for d in range(1, W):
        pl.semaphore_signal(barrier, inc=1, device_id={"wide": up_peer(d)}, device_id_type=MESH)
    for d in range(1, N):
        pl.semaphore_signal(
            barrier, inc=1, device_id={"narrow": lax.rem(nar + d, N)}, device_id_type=MESH
        )
    pl.semaphore_wait(barrier, W - 1 + N - 1)

    def request(d):
        rows = pl.ds(d * CR, CR)
        return pltpu.make_async_remote_copy(
            src_ref=sb.at[rows], dst_ref=rb.at[rows], send_sem=s1.at[d], recv_sem=r1.at[d],
            device_id={"wide": up_peer(d)}, device_id_type=MESH,
        )

    def answer(d):
        rows = pl.ds(d * CR, CR)
        return pltpu.make_async_remote_copy(
            src_ref=sb2.at[rows], dst_ref=rq.at[rows], send_sem=s2.at[d], recv_sem=r2.at[d],
            device_id={"wide": down_peer(d)}, device_id_type=MESH,
        )

    def request_scale(d):
        rows = pl.ds(d * R, R)
        return pltpu.make_async_remote_copy(
            src_ref=ss.at[rows], dst_ref=rs1.at[rows], send_sem=s6.at[d], recv_sem=r6.at[d],
            device_id={"wide": up_peer(d)}, device_id_type=MESH,
        )

    def answer_scale(d):
        rows = pl.ds(d * R, R)
        return pltpu.make_async_remote_copy(
            src_ref=ss2.at[rows], dst_ref=rs2.at[rows], send_sem=s7.at[d], recv_sem=r7.at[d],
            device_id={"wide": down_peer(d)}, device_id_type=MESH,
        )

    lane = lax.broadcasted_iota(jnp.int32, (R, BS), 1)

    def scatter(d):
        return pltpu.make_async_remote_copy(
            src_ref=pb.at[pl.ds(lax.rem(nar + d, N) * PR, PR)], dst_ref=rs.at[d],
            send_sem=s3.at[d], recv_sem=r3.at[d],
            device_id={"narrow": lax.rem(nar + d, N)}, device_id_type=MESH,
        )

    def gather(d):
        mine = pl.ds(nar * PR, PR)
        return pltpu.make_async_remote_copy(
            src_ref=out16, dst_ref=all16.at[mine], send_sem=s4.at[d], recv_sem=r4.at[d],
            device_id={"narrow": lax.rem(nar + d, N)}, device_id_type=MESH,
        )

    def gathered(d):
        theirs = pl.ds(lax.rem(nar - d + N, N) * PR, PR)
        return pltpu.make_async_remote_copy(
            src_ref=out16, dst_ref=all16.at[theirs], send_sem=s4.at[d], recv_sem=r4.at[d],
            device_id={"narrow": lax.rem(nar + d, N)}, device_id_type=MESH,
        )

    def scatter_scale(d):
        return pltpu.make_async_remote_copy(
            src_ref=psc.at[d], dst_ref=rsc.at[d], send_sem=s8.at[d], recv_sem=r8.at[d],
            device_id={"narrow": lax.rem(nar + d, N)}, device_id_type=MESH,
        )

    def gather_scale(d, slot):
        return pltpu.make_async_remote_copy(
            src_ref=osc, dst_ref=asc.at[slot], send_sem=s9.at[d], recv_sem=r9.at[d],
            device_id={"narrow": lax.rem(nar + d, N)}, device_id_type=MESH,
        )

    lane8 = lax.broadcasted_iota(jnp.int32, (8, BS), 1)

    def gram_copy(d):
        return pltpu.make_async_remote_copy(
            src_ref=gs, dst_ref=gr.at[d], send_sem=s5.at[d], recv_sem=r5.at[d],
            device_id={"wide": up_peer(d)}, device_id_type=MESH,
        )

    def gram_sum(value):
        gs[:, : 2 * R] = value
        gr[0, :, : 2 * R] = value
        for d in range(1, W):
            gram_copy(d).start()
        for d in range(1, W):
            gram_copy(d).wait_recv()
        summed = jnp.zeros((2 * R, 2 * R), jnp.float32)
        for s in range(W):
            summed += gr[lax.rem(me - s + W, W)][:, : 2 * R]
        for d in range(1, W):
            gram_copy(d).wait_send()
        return summed / total

    gs[...] = jnp.zeros_like(gs)
    xs[:R, :] = q_ref[...]
    xs[R:, :] = jnp.zeros((R, B * BS), jnp.float32)
    prev[...] = jnp.zeros_like(prev)
    up[...] = jnp.zeros_like(up)
    start = gram_sum(dot_nt(xs[...], xs[...], HIGH))
    _, _, inverse0 = factor_of(start[:R, :R], R)
    xs[:R, :] = dot32(inverse0, q_ref[...])

    def step(k, carry):
        for b in range(B):
            value = xs[:R, b * BS : (b + 1) * BS]
            blocks[b] = value
            whole, unit_of = coded(value)
            coded_blocks[b] = whole
            scales[b] = jnp.broadcast_to(unit_of, (R, BS))
        for d in range(W):
            spread = jnp.zeros((R, BS), jnp.float32)
            for c in range(C):
                value = coded_blocks[local[d * C + c]]
                (rb if d == 0 else sb)[pl.ds((d * C + c) * R, R), :] = value
                spread = jnp.where(lane == c, scales[local[d * C + c]], spread)
            (rs1 if d == 0 else ss)[pl.ds(d * R, R), :] = spread
            if d:
                request(d).start()
                request_scale(d).start()

        def group(d, carry):
            @pl.when(d > 0)
            def _():
                request(d).wait_recv()
                request_scale(d).wait_recv()

            scale_rows = pl.ds(pl.multiple_of(d * R, R), R)
            scale = rs1[scale_rows, :]
            spread = jnp.zeros((R, BS), jnp.float32)
            for c in range(C):
                p = d * C + c
                rows = pl.ds(pl.multiple_of(p * R, R), R)
                tile = tiles[p]
                high, low = split(number(rb[rows, :]))
                left = jnp.concatenate(
                    [
                        jnp.concatenate([high, high], axis=1),
                        jnp.concatenate([low, jnp.zeros_like(low)], axis=1),
                    ],
                    axis=0,
                )
                both = dot_nt(left, tile)
                tf[rows, :] = (both[:R] + both[R:]) * scale[:, c : c + 1]
                high, low = split(blocks[first[p]])
                both = jnp.dot(
                    jnp.concatenate([high, low], axis=0), tile, preferred_element_type=jnp.float32
                )
                whole, unit_of = coded(both[:R, :BS] + both[R:, :BS] + both[:R, BS:])
                sb2[rows, :] = whole
                spread = jnp.where(lane == c, unit_of, spread)
            ss2[scale_rows, :] = spread

            @pl.when(d > 0)
            def _():
                answer(d).start()
                answer_scale(d).start()

            return carry

        lax.fori_loop(0, W, group, 0)
        for d in range(W):
            if d:
                answer(d).wait_recv()
                answer_scale(d).wait_recv()
            scale = (rs2 if d else ss2)[pl.ds(d * R, R), :]
            for c in range(C):
                rows = pl.ds((d * C + c) * R, R)
                rb2[rows, :] = number((rq if d else sb2)[rows, :]) * scale[:, c : c + 1]

        one_hot = owners[...]
        for n in range(1, N + 1):
            part = lax.rem(nar + n, N)
            spread = jnp.zeros((8, BS), jnp.float32)
            for q in range(RN):
                r = part * RN + q
                x = jnp.concatenate(
                    [tf[pl.ds(r, W * C, stride=R), :], rb2[pl.ds(r, W * C, stride=R), :]], axis=0
                )
                high, low = split(x)
                value = jnp.dot(
                    one_hot,
                    jnp.concatenate([high, low], axis=0),
                    preferred_element_type=jnp.float32,
                )
                if n == N:
                    acc[pl.ds(q * B, B), :] = value
                else:
                    whole, unit_of = coded(value, (0, 1))
                    pb[pl.ds(pl.multiple_of(part * PR + q * B, B), B), :] = whole
                    spread = jnp.where(lane8 == q, unit_of, spread)
            if n < N:
                psc[n] = spread
                scatter(n).start()
                scatter_scale(n).start()
        for d in range(1, N):
            scatter(d).wait_recv()
            scatter_scale(d).wait_recv()
        spread = jnp.zeros((8, BS), jnp.float32)
        for q in range(RN):
            rows = pl.ds(q * B, B)
            value = acc[rows, :]
            for d in range(1, N):
                value += number(rs[d, rows, :]) * rsc[d][:1, q : q + 1]
            whole, unit_of = coded(value, (0, 1))
            out16[rows, :] = whole
            all16[pl.ds(pl.multiple_of(nar * PR + q * B, B), B), :] = whole
            spread = jnp.where(lane8 == q, unit_of, spread)
        osc[...] = spread
        asc[nar] = spread
        for d in range(1, N):
            gather(d).start()
            gather_scale(d, nar).start()
        for d in range(1, N):
            gathered(d).wait_recv()
            gather_scale(d, lax.rem(nar - d + N, N)).wait_recv()
        for r in range(R):
            rows = pl.ds(r * B, B)
            unit_of = asc[r // RN][:1, r % RN : r % RN + 1]
            ag[rows, :] = number(all16[rows, :]) * unit_of

        for b in range(B):
            xs[R:, b * BS : (b + 1) * BS] = ag[pl.ds(b, R, stride=B), :]
        xs[R:, :] = xs[R:, :] - dot32(up[...], prev[...])
        summed = gram_sum(dot_nt(xs[...], xs[...], HIGH))
        basis_gram = summed[:R, :R]
        along = summed[:R, R:]
        along_t = summed[R:, :R]
        raw = summed[R:, R:]
        gram = raw - 2.0 * dot32(along_t, along) + dot32(along_t, dot32(basis_gram, along))
        lower, upper, inverse = factor_of(gram, R)
        coef[k, 0] = along
        coef[k, 1] = lower
        prev[...] = xs[:R, :]
        up[...] = upper
        mix = jnp.concatenate([-dot32(inverse, along_t), inverse], axis=1)
        xs[:R, :] = dot32(mix, xs[...])

        for d in range(1, W):
            request(d).wait_send()
            answer(d).wait_send()
            request_scale(d).wait_send()
            answer_scale(d).wait_send()
        for d in range(1, N):
            scatter(d).wait_send()
            gather(d).wait_send()
            scatter_scale(d).wait_send()
            gather_scale(d, nar).wait_send()
        return carry

    lax.fori_loop(0, STEPS, step, 0)
    out[...] = xs[:R, :]


def quarter_scale(code):
    return jnp.exp(code.astype(jnp.float32) * (1.0 / LOG_STEPS))


def packed(values):
    top = jnp.abs(values[0])
    for value in values[1:]:
        top = jnp.maximum(top, jnp.abs(value))
    top = jnp.maximum(jnp.max(top, axis=1, keepdims=True), 1e-30)
    whole = jnp.ceil(jnp.log(top) * LOG_STEPS).astype(jnp.int32)
    whole = jnp.broadcast_to(whole, values[0].shape)
    factor = LEVELS / quarter_scale(whole)
    out = [
        jnp.clip(jnp.round(value * factor), -LEVELS, LEVELS).astype(jnp.int32).astype(jnp.int16)
        for value in values
    ]
    return out + [whole.astype(jnp.int16)]


SLOTS = 5
Z_ROWS = 48
PARTS = 4


def fused_kernel(dims, names, points, q_ref, pairs_ref, out, coef, *refs):
    W, N, C, R, B, F, total = dims
    s_ = dict(zip(names, refs))
    (unit, uq0, uq1, uq2, uq3, uq4, kt, tf1, tf2, vo, vr, rep, perm, shift, yt, zt, oht1, oht2, oh1, oh2, lv, ls, idx_i, idx_j, n2, w2, o1n, o1w, i1n, i1w,
     y1, y2, gs, gn, gt, gw, fin, qc, pv, wp, zp, at, inv, up) = (s_[n] for n in DATA)
    sem = s_
    uq = (uq0, uq1, uq2, uq3, uq4)
    QR = BS // N
    JQ = B // N
    HALF = W * C
    me = lax.axis_index("wide")
    nar = lax.axis_index("narrow")
    z, x = lax.div(me, 2), lax.rem(me, 2)
    h = lax.div(z, 2)
    e = lax.rem(z, 2)
    cd = (1 - h) * (3 - z) + h * (z - 2)
    cs = (1 - h) * (z + 2) + h * (3 - z)
    ax = 1 - x
    side = z + 1 - 2 * e
    XN = 2 * z + ax
    SRC = [XN, 2 * cs + x, 2 * cs + ax, 2 * side + (1 - e) * ax + e * x]
    DST = [XN, 2 * cd + x, 2 * cd + ax, 2 * side + (1 - e) * x + e * ax]
    GROUP = [me] + SRC
    lane = lax.broadcasted_iota(jnp.int32, (R, BS), 1)
    lane8 = lax.broadcasted_iota(jnp.int32, (8, BS), 1)
    sub8 = lax.broadcasted_iota(jnp.int32, (8, BS), 0)

    def slot_is(s, lanes=None):
        lanes = lane if lanes is None else lanes
        return (lanes >= s * QR) & (lanes < s * QR + QR)

    def filled(value):
        value = value + pltpu.roll(value, QR, 1)
        return value + pltpu.roll(value, 2 * QR, 1)

    def remote(src, dst, name, at_, where):
        return pltpu.make_async_remote_copy(
            src_ref=src, dst_ref=dst, send_sem=sem["s_" + name].at[at_], recv_sem=sem["r_" + name].at[at_],
            device_id=where, device_id_type=MESH,
        )

    def wide(d):
        return {"wide": d}

    def nearby(d):
        return {"narrow": lax.rem(nar + d, N)}

    def behind(d):
        return lax.rem(nar - d + N, N)

    PART = B // PARTS

    def part(s, t):
        return uq[s].at[pl.ds(t * PART, PART)]

    def hop_x(t):
        return remote(part(0, t), part(1, t), "px", t, wide(XN))

    def hop_c(t):
        return remote(part(0, t), part(2, t), "pc", t, wide(DST[1]))

    def hop_f(t):
        return remote(part(2, t), part(3, t), "pf", t, wide(XN))

    def hop_a(t, s=0):
        return remote(part(s, t), part(4, t), "pa", t, wide(2 * side + x))

    def list_near(d):
        return remote(pairs_ref, lv.at[0, nar], "ln", d, nearby(d))

    def list_wide(d):
        return remote(lv.at[0], lv.at[d], "lw", d, wide(DST[d]))

    def vec_near(k, d):
        return remote(n2.at[k, nar], n2.at[k, nar], "vn", (k, d), nearby(d))

    def vec_near_in(k, d):
        place = n2.at[k, behind(d)]
        return remote(place, place, "vn", (k, d), nearby(d))

    def vec_wide(k, d):
        return remote(n2.at[k, nar], w2.at[k, d], "vw", (k, d), wide(DST[d]))

    def sum_near(k, d):
        return remote(o1n.at[k, d], i1n.at[k, d], "sn", (k, d), nearby(d))

    def sum_wide(k, d):
        return remote(o1w.at[k, d], i1w.at[k, d], "sw", (k, d), wide(SRC[d]))

    def gram_near(k, d):
        return remote(gs.at[k], gn.at[k, nar], "gn", (k, d), nearby(d))

    def gram_near_in(k, d):
        place = gn.at[k, behind(d)]
        return remote(place, place, "gn", (k, d), nearby(d))

    def gram_wide(k, d):
        return remote(gt.at[k], gw.at[k, me], "gw", (k, d), wide(lax.rem(me + d, W)))

    def gram_wide_in(k, d):
        place = gw.at[k, lax.rem(me - d + W, W)]
        return remote(place, place, "gw", (k, d), wide(lax.rem(me + d, W)))

    def fin_near(d):
        return remote(fin.at[nar], fin.at[nar], "fn", d, nearby(d))

    def fin_near_in(d):
        place = fin.at[behind(d)]
        return remote(place, place, "fn", d, nearby(d))

    barrier = pltpu.get_barrier_semaphore()
    for d in range(1, W):
        pl.semaphore_signal(barrier, inc=1, device_id=wide(lax.rem(me + d, W)), device_id_type=MESH)
    for d in range(1, N):
        pl.semaphore_signal(barrier, inc=1, device_id=nearby(d), device_id_type=MESH)

    def normalise(b, carry):
        unit[b] = unit_rows(points[pl.ds(pl.multiple_of(b * BS, BS), BS), :])
        return carry

    def quarter(b, carry):
        uq0[b] = unit_rows(points[pl.ds(pl.multiple_of(b * BS + nar * QR, QR), QR), :])
        return carry

    lax.fori_loop(0, B, quarter, 0, unroll=4)

    def square(x_):
        four = jnp.concatenate([x_] * (BS // (2 * R)), axis=0)
        full = dot_nt(x_, four, HIGH)
        small = jnp.zeros((8, BS), jnp.float32)
        for a in range(2 * R // 8):
            small = jnp.where(slot_is(a, lane8), full[8 * a : 8 * a + 8], small)
        return small

    def gram_value(k):
        total_ = gw[k, 0]
        for d in range(1, W):
            total_ = total_ + gw[k, d]
        rows = [total_] + [pltpu.roll(total_, BS - a * 2 * R, 1) for a in range(1, 2 * R // 8)]
        return jnp.concatenate(rows, axis=0)[:, : 2 * R] / total

    def gram_send(k):
        gw[k, me] = gt[k]
        for d in range(1, W):
            gram_wide(k, d).start()

    def gram_collect(k):
        for d in range(1, N):
            gram_near_in(k, d).wait_recv()
        value = gn[k, 0]
        for d in range(1, N):
            value = value + gn[k, d]
        gt[k] = value
        gram_send(k)

    def gram_start(k):
        value = square(jnp.concatenate([qc[...], wp[...]], axis=0))
        gs[k] = value
        gn[k, nar] = value
        for d in range(1, N):
            gram_near(k, d).start()

    def gram_finish(k):
        for d in range(1, W):
            gram_wide_in(k, d).wait_recv()
        summed = gram_value(k)
        along = summed[:R, R:]
        along_t = summed[R:, :R]
        gram = summed[R:, R:] - 2.0 * dot32(along_t, along) + dot32(along_t, dot32(summed[:R, :R], along))
        lower, upper, inverse = factor_of(gram, R)
        coef[k - 1, 0] = along
        coef[k - 1, 1] = lower
        at[...] = along_t
        inv[...] = inverse
        up[...] = upper
        pv[...] = qc[...]
        qc[...] = dot32(inverse, wp[...] - dot32(along_t, qc[...]))

    pl.semaphore_wait(barrier, W - 1 + N - 1)

    for t in range(PARTS):
        hop_x(t).start()
        hop_c(t).start()

        @pl.when(e == 0)
        def _():
            hop_a(t).start()

    lv[0, nar] = pairs_ref[...]
    for d in range(1, N):
        list_near(d).start()
    q_all = q_ref[...]
    gt[0] = square(jnp.concatenate([q_all, q_all], axis=0))
    gram_send(0)
    lax.fori_loop(0, B, normalise, 0, unroll=2)

    def places(rows, columns, of):
        row = lax.broadcasted_iota(jnp.int32, (rows, columns), 0)
        column = lax.broadcasted_iota(jnp.int32, (rows, columns), 1)
        return (row == of(column)).astype(jnp.float32).astype(jnp.bfloat16)

    rep[...] = places(BS, N * BS, lambda l: (l // BS) * QR + (l & (QR - 1)))
    perm[...] = places(
        N * BS, N * BS, lambda l: ((l // QR) & (N - 1)) * BS + (l // BS) * QR + (l & (QR - 1))
    )
    for a in range(N):
        shift[a * BS : (a + 1) * BS, :] = places(
            BS, BS, lambda l: ((l // QR + N - a) & (N - 1)) * QR + (l & (QR - 1))
        )

    for d in range(1, N):
        place = lv.at[0, behind(d)]
        remote(place, place, "ln", d, nearby(d)).wait_recv()
    for d in range(1, 4):
        list_wide(d).start()

    for jq in range(JQ):
        value = jnp.zeros((R, BS), jnp.float32)
        for s in range(N):
            b = N * jq + s
            one = filled(jnp.where(slot_is(nar), q_ref[:, b * BS : (b + 1) * BS], 0.0))
            value = jnp.where(slot_is(s), one, value)
        wp[:, jq * BS : (jq + 1) * BS] = value

    for d in range(1, W):
        gram_wide_in(0, d).wait_recv()
    _, _, inverse0 = factor_of(gram_value(0)[:R, :R], R)
    qc[...] = dot32(inverse0, wp[...])
    for ref in (pv, zp, at, up):
        ref[...] = jnp.zeros_like(ref)
    inv[...] = (
        lax.broadcasted_iota(jnp.int32, (R, R), 0) == lax.broadcasted_iota(jnp.int32, (R, R), 1)
    ).astype(jnp.float32)

    def lanes_of(ref):
        return [ref[:, jq * BS : (jq + 1) * BS] for jq in range(JQ)]

    def vec_send(k, ref):
        for jq, value in enumerate(packed(lanes_of(ref))):
            n2[k, nar, jq * R : (jq + 1) * R, :] = value
        for d in range(1, N):
            vec_near(k, d).start()
        for d in range(4):
            vec_wide(k, d).start()

    vec_send(0, qc)

    for d in range(1, 4):
        remote(lv.at[d], lv.at[d], "lw", d, wide(DST[d])).wait_recv()
    local = pltpu.make_async_copy(lv, ls, sem["m_ls"])
    local.start()
    local.wait()

    kinds = []
    for s in range(SLOTS):
        kinds.append((s, 0))
        if s > 1:
            kinds.append((s, 1))

    for at_kind, (s, kind) in enumerate(kinds):
        other = GROUP[s]

        def indices(mq, carry):
            ch = at_kind * N + mq
            vi = jnp.zeros((8, BS), jnp.int32)
            vj = jnp.zeros((8, BS), jnp.int32)
            for c in range(C):
                if kind == 0:
                    i = ls[0, mq, 0, other * C + c]
                    j = ls[0, mq, 0, HALF + other * C + c]
                else:
                    j = ls[s - 1, mq, 0, me * C + c]
                    i = ls[s - 1, mq, 0, HALF + me * C + c]
                idx_i[ch * C + c] = i
                idx_j[ch * C + c] = j
                vi = jnp.where(sub8 == c, i, vi)
                vj = jnp.where(sub8 == c, j, vj)
            rows = pl.ds(pl.multiple_of(ch * C, C), C)
            row = (vi & (N - 1)) * JQ + vi // N
            oht1[rows, :] = (row == lane8).astype(jnp.float32)
            row = ((vj + N - (sub8 & (N - 1))) & (N - 1)) * Z_ROWS + s * JQ + vj // N
            oht2[rows, :BS] = (row == lane8).astype(jnp.float32)
            oht2[rows, BS:] = (row == lane8 + BS).astype(jnp.float32)
            return carry

        lax.fori_loop(0, N, indices, 0)

    turned = jnp.transpose(oht1[...])[: oh1.shape[0]].astype(jnp.bfloat16)
    oh1[...] = jnp.concatenate([turned, turned], axis=1)
    turned = jnp.transpose(oht2[...])[: oh2.shape[0]].astype(jnp.bfloat16)
    oh2[...] = jnp.concatenate([turned, turned], axis=1)

    def tiles_of(want):
        for at_kind, (s, kind) in enumerate(kinds):
            if s != want:
                continue

            def make(mq, carry):
                ch = at_kind * N + mq
                for c in range(C):
                    p = ch * C + c
                    sim = dot_nt(uq[s][idx_j[p]], unit[idx_i[p]])
                    high, low = split(jnp.exp(KERNEL_FACTOR * (sim - 1.0)))
                    rows = pl.ds(pl.multiple_of(p * QR, QR), QR)
                    kt[rows, :BS] = high
                    kt[rows, BS:] = low
                return carry

            lax.fori_loop(0, N, make, 0)

    tiles_of(0)
    for t in range(PARTS):
        hop_x(t).wait_recv()

        @pl.when(e == 1)
        def _():
            hop_a(t, 1).start()

        hop_c(t).wait_recv()
        hop_f(t).start()
    tiles_of(1)
    tiles_of(2)
    for t in range(PARTS):
        hop_a(t).wait_recv()
    tiles_of(4)
    for t in range(PARTS):
        hop_f(t).wait_recv()
    tiles_of(3)

    chunks = len(kinds) * N
    slots_of_chunk = [s for s, _ in kinds for _ in range(N)]

    def unpacked(ref, k, d):
        scale = quarter_scale(ref[k, d, JQ * R : (JQ + 1) * R, :].astype(jnp.int32)) * (1.0 / LEVELS)
        return [number(ref[k, d, jq * R : (jq + 1) * R, :]) * scale for jq in range(JQ)]

    def both(value):
        return jnp.concatenate(split(value), axis=0)

    def scatter(tf, one_hot, keep):
        for r in range(0, R, 2):
            columns = []
            for q in range(2):
                high, low = split(tf[pl.ds(r + q, chunks * C, stride=R), :])
                columns.append(jnp.concatenate([high, low], axis=0))
            value = jnp.dot(
                one_hot[...], jnp.concatenate(columns, axis=1), preferred_element_type=jnp.float32
            )
            keep(r, value[:, :BS])
            keep(r + 1, value[:, BS:])

    def moved(value, matrix):
        rows = value.shape[0]
        value = jnp.dot(both(value), matrix[...], preferred_element_type=jnp.float32)
        return value[:rows] + value[rows:]

    def step(k, carry):
        for d in range(1, N):
            vec_near_in(k, d).wait_recv()
        quarters = [unpacked(n2, k, q) for q in range(N)]
        pieces = [
            jnp.concatenate([both(quarters[q][jq]) for q in range(N)], axis=1) for jq in range(JQ)
        ]
        value = jnp.dot(jnp.concatenate(pieces, axis=0), perm[...], preferred_element_type=jnp.float32)
        value = value.astype(jnp.bfloat16)
        for jq in range(JQ):
            for s in range(N):
                vo[jq * N + s] = value[2 * R * jq : 2 * R * (jq + 1), s * BS : (s + 1) * BS]
        mine = unpacked(n2, k, nar)

        def keep_remote(s, values):
            value = jnp.dot(
                jnp.concatenate([both(v) for v in values], axis=0), rep[...],
                preferred_element_type=jnp.float32,
            ).astype(jnp.bfloat16)
            for jq in range(JQ):
                for b in range(N):
                    vr[s * B + jq * N + b] = value[2 * R * jq : 2 * R * (jq + 1), b * BS : (b + 1) * BS]

        keep_remote(0, mine)

        @pl.when(k > 0)
        def _():
            gram_collect(k)

        def second(ch, carry):
            left = jnp.concatenate([vo[idx_i[ch * C + c]] for c in range(C)], axis=0)
            tile = kt[pl.ds(pl.multiple_of(ch * C * QR, C * QR), C * QR), :]
            full = dot_nt(jnp.concatenate([left, left], axis=1), tile)
            for c in range(C):
                columns = slice((c // N) * BS, (c // N + 1) * BS)
                value = full[2 * R * c : 2 * R * c + R, columns] + full[2 * R * c + R : 2 * R * (c + 1), columns]
                value = jnp.where(slot_is(c % N), value, 0.0)
                tf2[pl.ds(pl.multiple_of((ch * C + c) * R, R), R), :] = value
            return carry

        lax.fori_loop(0, chunks, second, 0, unroll=2)

        def keep2(r, value):
            for a in range(N):
                zt[r * SLOTS * JQ : (r + 1) * SLOTS * JQ, a * BS : (a + 1) * BS] = (
                    value[a * Z_ROWS : a * Z_ROWS + SLOTS * JQ]
                )

        scatter(tf2, oh2, keep2)
        batch = R // 4
        for first_r in range(0, R, batch):
            value = moved(zt[first_r * SLOTS * JQ : (first_r + batch) * SLOTS * JQ, :], shift)
            for r in range(batch):
                for s in range(SLOTS):
                    place = (r * SLOTS + s) * JQ
                    y2[s, pl.ds(first_r + r, JQ, stride=R), :] = value[place : place + JQ]
        for d in range(4):
            for jq, value in enumerate(packed([y2[d + 1, jq * R : (jq + 1) * R, :] for jq in range(JQ)])):
                o1w[k, d, jq * R : (jq + 1) * R, :] = value
            sum_wide(k, d).start()

        for d in range(4):
            remote(w2.at[k, d], w2.at[k, d], "vw", (k, d), wide(DST[d])).wait_recv()
            keep_remote(d + 1, unpacked(w2, k, d))

        for s in range(SLOTS):
            first_chunk = slots_of_chunk.index(s)

            def first(ch, carry):
                left = []
                for c in range(C):
                    value = vr[s * B + idx_j[ch * C + c]]
                    value = jnp.where(slot_is(c % N, lane2), value, jnp.zeros_like(value))
                    pieces = [jnp.zeros_like(value)] * (C // N)
                    pieces[c // N] = value
                    left.append(jnp.concatenate(pieces, axis=1))
                tile = kt[pl.ds(pl.multiple_of(ch * C * QR, C * QR), C * QR), :]
                full = jnp.dot(jnp.concatenate(left, axis=0), tile, preferred_element_type=jnp.float32)
                for c in range(C):
                    high = full[2 * R * c : 2 * R * c + R]
                    low = full[2 * R * c + R : 2 * R * (c + 1)]
                    tf1[pl.ds(pl.multiple_of((ch * C + c) * R, R), R), :] = (
                        high[:, :BS] + high[:, BS:] + low[:, :BS]
                    )
                return carry

            lax.fori_loop(first_chunk, first_chunk + slots_of_chunk.count(s), first, 0, unroll=2)

        def keep1(r, value):
            for s in range(N):
                yt[r * JQ : (r + 1) * JQ, s * BS : (s + 1) * BS] = value[s * JQ : (s + 1) * JQ]

        scatter(tf1, oh1, keep1)
        value = moved(yt[...], perm)
        for r in range(R):
            for q in range(N):
                y1[q, pl.ds(r, JQ, stride=R), :] = value[r * JQ : (r + 1) * JQ, q * BS : (q + 1) * BS]

        for d in range(1, N):
            to = lax.rem(nar + d, N)
            for jq, value in enumerate(packed([y1[to, jq * R : (jq + 1) * R, :] for jq in range(JQ)])):
                o1n[k, d, jq * R : (jq + 1) * R, :] = value
            sum_near(k, d).start()

        @pl.when(k > 0)
        def _():
            gram_finish(k)

        image = [y1[nar, jq * R : (jq + 1) * R, :] + y2[0, jq * R : (jq + 1) * R, :] for jq in range(JQ)]
        for d in range(4):
            sum_wide(k, d).wait_recv()
            image = [a + b for a, b in zip(image, unpacked(i1w, k, d))]
        for d in range(1, N):
            sum_near(k, d).wait_recv()
            image = [a + b for a, b in zip(image, unpacked(i1n, k, d))]
        image = jnp.concatenate(image, axis=1)
        image = dot32(inv[...], image - dot32(at[...], zp[...]))
        zp[...] = image
        wp[...] = image - dot32(up[...], pv[...])

        @pl.when(k < STEPS - 1)
        def _():
            vec_send(k + 1, wp)

        gram_start(k + 1)
        return carry

    lane2 = lax.broadcasted_iota(jnp.int32, (2 * R, BS), 1)
    lax.fori_loop(0, STEPS, step, 0)
    gram_collect(STEPS)
    gram_finish(STEPS)
    for jq, value in enumerate(lanes_of(qc)):
        fin[nar, jq * R : (jq + 1) * R, :] = value
    for d in range(1, N):
        fin_near(d).start()
    for d in range(1, N):
        fin_near_in(d).wait_recv()
    value = moved(jnp.concatenate([fin[q] for q in range(N)], axis=1), perm)
    for jq in range(JQ):
        for s in range(N):
            b = jq * N + s
            out[:, b * BS : (b + 1) * BS] = value[jq * R : (jq + 1) * R, s * BS : (s + 1) * BS]

    for t in range(PARTS):
        hop_x(t).wait_send()
        hop_c(t).wait_send()
        hop_a(t).wait_send()
        hop_f(t).wait_send()
    for d in range(1, N):
        list_near(d).wait_send()
        fin_near(d).wait_send()
    for d in range(1, 4):
        list_wide(d).wait_send()
    for d in range(1, W):
        gram_wide(0, d).wait_send()
    for k in range(STEPS):
        for d in range(1, N):
            vec_near(k, d).wait_send()
            sum_near(k, d).wait_send()
            gram_near(k + 1, d).wait_send()
        for d in range(4):
            vec_wide(k, d).wait_send()
            sum_wide(k, d).wait_send()
        for d in range(1, W):
            gram_wide(k + 1, d).wait_send()


DATA = (
    "unit", "uq0", "uq1", "uq2", "uq3", "uq4", "kt", "tf1", "tf2", "vo", "vr", "rep", "perm", "shift", "yt", "zt", "oht1", "oht2",
    "oh1", "oh2", "lv", "ls", "idx_i", "idx_j", "n2", "w2", "o1n", "o1w", "i1n", "i1w", "y1", "y2",
    "gs", "gn", "gt", "gw", "fin", "qc", "pv", "wp", "zp", "at", "inv", "up",
)


def fused(points, q_init, pairs, W, N):
    R, cols = q_init.shape
    F = points.shape[1]
    B = cols // BS
    pair_count = pairs.shape[1]
    C = pair_count // W
    QR, JQ = BS // N, B // N
    P_ = (SLOTS + SLOTS - 2) * N * C
    f32, bf16, i16, i32 = jnp.float32, jnp.bfloat16, jnp.int16, jnp.int32
    V = pltpu.VMEM
    message = ((JQ + 1) * R, BS)
    rounds = STEPS + 1
    columns = JQ * BS
    shapes = {
        "unit": V((B, BS, F), bf16), **{f"uq{s}": V((B, QR, F), bf16) for s in range(SLOTS)}, "kt": V((P_ * QR, 2 * BS), bf16),
        "tf1": V((P_ * R, BS), f32), "tf2": V((P_ * R, BS), f32),
        "vo": V((B, 2 * R, BS), bf16), "vr": V((SLOTS * B, 2 * R, BS), bf16),
        "oht1": V((P_, BS), f32), "oht2": V((P_, 2 * BS), f32),
        "rep": V((BS, N * BS), bf16), "perm": V((N * BS, N * BS), bf16), "shift": V((N * BS, BS), bf16),
        "yt": V((R * JQ, N * BS), f32), "zt": V((R * SLOTS * JQ, N * BS), f32),
        "oh1": V((B, 2 * P_), bf16), "oh2": V((N * Z_ROWS, 2 * P_), bf16),
        "lv": V((4, N, 1, 2 * pair_count), i32), "ls": pltpu.SMEM((4, N, 1, 2 * pair_count), i32),
        "idx_i": pltpu.SMEM((P_,), i32), "idx_j": pltpu.SMEM((P_,), i32),
        "n2": V((STEPS, N) + message, i16), "w2": V((STEPS, 4) + message, i16),
        "o1n": V((STEPS, N) + message, i16), "o1w": V((STEPS, 4) + message, i16),
        "i1n": V((STEPS, N) + message, i16), "i1w": V((STEPS, 4) + message, i16),
        "y1": V((N, JQ * R, BS), f32), "y2": V((SLOTS, JQ * R, BS), f32),
        "gs": V((rounds, 8, BS), f32), "gn": V((rounds, N, 8, BS), f32),
        "gt": V((rounds, 8, BS), f32), "gw": V((rounds, W, 8, BS), f32),
        "fin": V((N, JQ * R, BS), f32),
        "qc": V((R, columns), f32), "pv": V((R, columns), f32), "wp": V((R, columns), f32),
        "zp": V((R, columns), f32),
        "at": V((R, R), f32), "inv": V((R, R), f32), "up": V((R, R), f32),
    }
    sems = {
        "px": (PARTS,), "pc": (PARTS,), "pf": (PARTS,), "pa": (PARTS,), "ln": (N,), "lw": (4,),
        "vn": (STEPS, N), "vw": (STEPS, 4), "sn": (STEPS, N), "sw": (STEPS, 4),
        "gn": (rounds, N), "gw": (rounds, W), "fn": (N,),
    }
    names = list(DATA)
    scratch = [shapes[n] for n in DATA]
    for name, shape in sems.items():
        for way in "sr":
            names.append(way + "_" + name)
            scratch.append(pltpu.SemaphoreType.DMA(shape))
    names.append("m_ls")
    scratch.append(pltpu.SemaphoreType.DMA)
    vmem = pl.BlockSpec(memory_space=pltpu.VMEM)
    dims = (W, N, C, R, B, F, B * BS * W)
    return pl.pallas_call(
        functools.partial(fused_kernel, dims, tuple(names)),
        out_shape=(
            jax.ShapeDtypeStruct((R, cols), f32),
            jax.ShapeDtypeStruct((STEPS, 2, R, R), f32),
        ),
        in_specs=[vmem, vmem, vmem],
        out_specs=(vmem, vmem),
        scratch_shapes=scratch,
        compiler_params=pltpu.CompilerParams(collective_id=1, has_side_effects=True),
        name="fused",
    )(points, q_init, lax.rem(pairs, B).reshape(1, 2 * pair_count))


def lanczos(first, local, owners, tiles, q_init, wide_count, narrow_count, total):
    R, cols = q_init.shape
    B = cols // BS
    pair_count = first.shape[0]
    C = pair_count // wide_count
    dims = (wide_count, narrow_count, C, R, B, total)
    vmem = pl.BlockSpec(memory_space=pltpu.VMEM)
    smem = pl.BlockSpec(memory_space=pltpu.SMEM)
    f32 = jnp.float32
    pairs_buf = pltpu.VMEM((pair_count * R, BS), f32)
    coded_buf = pltpu.VMEM((pair_count * R, BS), jnp.int16)
    scale_buf = pltpu.VMEM((wide_count * R, BS), f32)
    part = R // narrow_count * B
    wide_sem = pltpu.SemaphoreType.DMA((wide_count,))
    narrow_sem = pltpu.SemaphoreType.DMA((narrow_count,))
    return pl.pallas_call(
        functools.partial(main_kernel, dims),
        out_shape=(
            jax.ShapeDtypeStruct((R, cols), f32),
            jax.ShapeDtypeStruct((STEPS, 2, R, R), f32),
        ),
        in_specs=[smem, smem, vmem, vmem, vmem],
        out_specs=(vmem, vmem),
        scratch_shapes=[
            coded_buf, coded_buf, coded_buf, coded_buf,
            scale_buf, scale_buf, scale_buf, scale_buf,
            pltpu.VMEM((B, R, BS), jnp.int16),
            pltpu.VMEM((B, R, BS), f32),
            pairs_buf, pairs_buf,
            pltpu.VMEM((R * B, BS), jnp.int16),
            pltpu.VMEM((narrow_count, part, BS), jnp.int16),
            pltpu.VMEM((R * B, BS), f32),
            pltpu.VMEM((part, BS), f32),
            pltpu.VMEM((part, BS), jnp.int16),
            pltpu.VMEM((R * B, BS), jnp.int16),
            pltpu.VMEM((narrow_count, 8, BS), f32),
            pltpu.VMEM((narrow_count, 8, BS), f32),
            pltpu.VMEM((8, BS), f32),
            pltpu.VMEM((narrow_count, 8, BS), f32),
            pltpu.VMEM((2 * R, cols), f32),
            pltpu.VMEM((B, R, BS), f32),
            pltpu.VMEM((R, cols), f32),
            pltpu.VMEM((R, R), f32),
            pltpu.VMEM((2 * R, BS), f32),
            pltpu.VMEM((wide_count, 2 * R, BS), f32),
            wide_sem, wide_sem, wide_sem, wide_sem,
            narrow_sem, narrow_sem, narrow_sem, narrow_sem,
            wide_sem, wide_sem, wide_sem, wide_sem, wide_sem, wide_sem,
            narrow_sem, narrow_sem, narrow_sem, narrow_sem,
        ],
        compiler_params=pltpu.CompilerParams(collective_id=0, has_side_effects=True),
        name="lanczos",
    )(first, local, owners, tiles, q_init)


def per_device(points, q_init, pairs):
    wide_count = lax.axis_size("wide")
    narrow_count = lax.axis_size("narrow")
    me = lax.axis_index("wide")
    own_blocks = points.shape[0] // BS
    width = points.shape[1]
    pair_count = pairs.shape[1]
    capacity = pair_count // wide_count
    if wide_count == 8 and narrow_count == 4 and own_blocks == 8 * narrow_count and capacity == 8:
        return fused(points, q_init, pairs, wide_count, narrow_count)
    total = own_blocks * BS * wide_count
    unit = unit_rows(points).reshape(own_blocks, BS, width)
    turn = jnp.arange(wide_count, dtype=jnp.int32)
    first_rows = (pairs[0] - me * own_blocks).reshape(wide_count, capacity)
    first = first_rows[(me - turn) % wide_count].reshape(pair_count)
    second = (pairs[1].reshape(wide_count, capacity) - turn[:, None] * own_blocks)
    every = lax.all_to_all(
        jnp.broadcast_to(second.reshape(1, pair_count), (wide_count, pair_count)),
        "wide", split_axis=0, concat_axis=0, tiled=True,
    ).reshape(wide_count, wide_count, capacity)
    local_ids = lax.dynamic_index_in_dim(every, me, axis=1, keepdims=False)
    local = local_ids[(me + turn) % wide_count].reshape(pair_count)
    targets = jnp.concatenate([first, local, first, local])
    owners = (jnp.arange(own_blocks, dtype=jnp.int32)[:, None] == targets[None, :]).astype(
        jnp.bfloat16
    )
    blocks = lax.all_to_all(
        unit[local_ids.reshape(pair_count)], "wide", split_axis=0, concat_axis=0, tiled=True
    ).reshape(wide_count, capacity, BS, width)
    tiles = make_tiles(jnp.reshape(me, (1,)).astype(jnp.int32), first, unit, blocks)
    return lanczos(first, local, owners, tiles, q_init, wide_count, narrow_count, total)


def solution(mesh):
    placed = (P("wide", None), P(None, "wide"), P(None, ("wide", "narrow")))
    return jax.shard_map(
        per_device, mesh=mesh, in_specs=placed, out_specs=(P(None, "wide"), P()), check_vma=False
    )
```

```python
import functools

import jax
import jax.numpy as jnp
from jax import lax
from jax.experimental import pallas as pl
from jax.experimental.pallas import tpu as pltpu
from jax.sharding import PartitionSpec as P

BS = 128
STEPS = 3
LEVELS = 32767.0
KERNEL_FACTOR = 3.0
EPSILON = 1e-06
LOG_STEPS = 256.0
HIGH = lax.Precision.HIGHEST
MESH = pl.DeviceIdType.MESH


def unit_rows(points):
    wide32 = points.astype(jnp.float32)
    scaled = wide32 * lax.rsqrt(jnp.sum(wide32 * wide32, axis=-1, keepdims=True) + EPSILON)
    return scaled.astype(jnp.bfloat16)


def split(x):
    high = x.astype(jnp.bfloat16)
    return high, (x - high.astype(jnp.float32)).astype(jnp.bfloat16)


def coded(x, axes=1):
    top = jnp.maximum(jnp.max(jnp.abs(x), axis=axes, keepdims=True), 1e-30)
    scaled = jnp.clip(jnp.round(x * (LEVELS / top)), -LEVELS, LEVELS)
    return scaled.astype(jnp.int32).astype(jnp.int16), top * (1.0 / LEVELS)


def number(x):
    return x.astype(jnp.int32).astype(jnp.float32)


def dot32(a, b):
    return jnp.dot(a, b, precision=HIGH, preferred_element_type=jnp.float32)


def dot_nt(a, b, precision=None):
    return lax.dot_general(
        a, b, (((1,), (1,)), ((), ())), precision=precision, preferred_element_type=jnp.float32
    )


def tiles_kernel(capacity, me_ref, first_ref, unit_ref, second_ref, out_ref):
    d = pl.program_id(0)
    for c in range(capacity):
        s = dot_nt(unit_ref[first_ref[d * capacity + c]], second_ref[0, c])
        high, low = split(jnp.exp(KERNEL_FACTOR * (s - 1.0)))
        out_ref[c, :, :BS] = high
        out_ref[c, :, BS:] = low


def make_tiles(me, first, unit, second):
    wide_count, capacity, _, width = second.shape
    own_blocks = unit.shape[0]
    spec = pltpu.PrefetchScalarGridSpec(
        num_scalar_prefetch=2,
        grid=(wide_count,),
        in_specs=[
            pl.BlockSpec((own_blocks, BS, width), lambda d, m, f: (0, 0, 0)),
            pl.BlockSpec(
                (1, capacity, BS, width),
                lambda d, m, f: (lax.rem(m[0] - d + wide_count, wide_count), 0, 0, 0),
            ),
        ],
        out_specs=pl.BlockSpec((capacity, BS, 2 * BS), lambda d, m, f: (d, 0, 0)),
    )
    return pl.pallas_call(
        functools.partial(tiles_kernel, capacity),
        grid_spec=spec,
        out_shape=jax.ShapeDtypeStruct((wide_count * capacity, BS, 2 * BS), jnp.bfloat16),
        name="tiles",
    )(me, first, unit, second)


def factor_of(gram, r):
    i = lax.broadcasted_iota(jnp.int32, (r, r), 0)
    j = lax.broadcasted_iota(jnp.int32, (r, r), 1)
    both_i = lax.broadcasted_iota(jnp.int32, (r, 2 * r), 0)
    m = jnp.concatenate([gram, (i == j).astype(jnp.float32)], axis=1)
    lower = jnp.zeros((r, r), jnp.float32)
    for k in range(r):
        inv = 1.0 / jnp.sqrt(m[k : k + 1, k : k + 1])
        row = m[k : k + 1, :] * inv
        col = m[:, k : k + 1] * inv
        lower = jnp.where((j == k) & (i >= k), col, lower)
        m = jnp.where(both_i == k, row, jnp.where(both_i > k, m - col * row, m))
    upper = jnp.where(j >= i, m[:, :r], 0.0)
    inverse = jnp.where(j <= i, m[:, r:], 0.0)
    return lower, upper, inverse


def main_kernel(
    dims, first, local, owners, tiles, q_ref, out, coef,
    sb, rb, sb2, rq, ss, rs1, ss2, rs2, coded_blocks, scales, rb2, tf, pb, rs, ag, acc, out16, all16, psc, rsc, osc, asc, xs, blocks, prev, up, gs, gr,
    s1, r1, s2, r2, s3, r3, s4, r4, s5, r5, s6, r6, s7, r7, s8, r8, s9, r9,
):
    W, N, C, R, B, total = dims
    CR = C * R
    RN = R // N
    PR = RN * B
    me = lax.axis_index("wide")
    nar = lax.axis_index("narrow")

    def up_peer(d):
        return lax.rem(me + d, W)

    def down_peer(d):
        return lax.rem(me - d + W, W)

    barrier = pltpu.get_barrier_semaphore()
    for d in range(1, W):
        pl.semaphore_signal(barrier, inc=1, device_id={"wide": up_peer(d)}, device_id_type=MESH)
    for d in range(1, N):
        pl.semaphore_signal(
            barrier, inc=1, device_id={"narrow": lax.rem(nar + d, N)}, device_id_type=MESH
        )
    pl.semaphore_wait(barrier, W - 1 + N - 1)

    def request(d):
        rows = pl.ds(d * CR, CR)
        return pltpu.make_async_remote_copy(
            src_ref=sb.at[rows], dst_ref=rb.at[rows], send_sem=s1.at[d], recv_sem=r1.at[d],
            device_id={"wide": up_peer(d)}, device_id_type=MESH,
        )

    def answer(d):
        rows = pl.ds(d * CR, CR)
        return pltpu.make_async_remote_copy(
            src_ref=sb2.at[rows], dst_ref=rq.at[rows], send_sem=s2.at[d], recv_sem=r2.at[d],
            device_id={"wide": down_peer(d)}, device_id_type=MESH,
        )

    def request_scale(d):
        rows = pl.ds(d * R, R)
        return pltpu.make_async_remote_copy(
            src_ref=ss.at[rows], dst_ref=rs1.at[rows], send_sem=s6.at[d], recv_sem=r6.at[d],
            device_id={"wide": up_peer(d)}, device_id_type=MESH,
        )

    def answer_scale(d):
        rows = pl.ds(d * R, R)
        return pltpu.make_async_remote_copy(
            src_ref=ss2.at[rows], dst_ref=rs2.at[rows], send_sem=s7.at[d], recv_sem=r7.at[d],
            device_id={"wide": down_peer(d)}, device_id_type=MESH,
        )

    lane = lax.broadcasted_iota(jnp.int32, (R, BS), 1)

    def scatter(d):
        return pltpu.make_async_remote_copy(
            src_ref=pb.at[pl.ds(lax.rem(nar + d, N) * PR, PR)], dst_ref=rs.at[d],
            send_sem=s3.at[d], recv_sem=r3.at[d],
            device_id={"narrow": lax.rem(nar + d, N)}, device_id_type=MESH,
        )

    def gather(d):
        mine = pl.ds(nar * PR, PR)
        return pltpu.make_async_remote_copy(
            src_ref=out16, dst_ref=all16.at[mine], send_sem=s4.at[d], recv_sem=r4.at[d],
            device_id={"narrow": lax.rem(nar + d, N)}, device_id_type=MESH,
        )

    def gathered(d):
        theirs = pl.ds(lax.rem(nar - d + N, N) * PR, PR)
        return pltpu.make_async_remote_copy(
            src_ref=out16, dst_ref=all16.at[theirs], send_sem=s4.at[d], recv_sem=r4.at[d],
            device_id={"narrow": lax.rem(nar + d, N)}, device_id_type=MESH,
        )

    def scatter_scale(d):
        return pltpu.make_async_remote_copy(
            src_ref=psc.at[d], dst_ref=rsc.at[d], send_sem=s8.at[d], recv_sem=r8.at[d],
            device_id={"narrow": lax.rem(nar + d, N)}, device_id_type=MESH,
        )

    def gather_scale(d, slot):
        return pltpu.make_async_remote_copy(
            src_ref=osc, dst_ref=asc.at[slot], send_sem=s9.at[d], recv_sem=r9.at[d],
            device_id={"narrow": lax.rem(nar + d, N)}, device_id_type=MESH,
        )

    lane8 = lax.broadcasted_iota(jnp.int32, (8, BS), 1)

    def gram_copy(d):
        return pltpu.make_async_remote_copy(
            src_ref=gs, dst_ref=gr.at[d], send_sem=s5.at[d], recv_sem=r5.at[d],
            device_id={"wide": up_peer(d)}, device_id_type=MESH,
        )

    def gram_sum(value):
        gs[:, : 2 * R] = value
        gr[0, :, : 2 * R] = value
        for d in range(1, W):
            gram_copy(d).start()
        for d in range(1, W):
            gram_copy(d).wait_recv()
        summed = jnp.zeros((2 * R, 2 * R), jnp.float32)
        for s in range(W):
            summed += gr[lax.rem(me - s + W, W)][:, : 2 * R]
        for d in range(1, W):
            gram_copy(d).wait_send()
        return summed / total

    gs[...] = jnp.zeros_like(gs)
    xs[:R, :] = q_ref[...]
    xs[R:, :] = jnp.zeros((R, B * BS), jnp.float32)
    prev[...] = jnp.zeros_like(prev)
    up[...] = jnp.zeros_like(up)
    start = gram_sum(dot_nt(xs[...], xs[...], HIGH))
    _, _, inverse0 = factor_of(start[:R, :R], R)
    xs[:R, :] = dot32(inverse0, q_ref[...])

    def step(k, carry):
        for b in range(B):
            value = xs[:R, b * BS : (b + 1) * BS]
            blocks[b] = value
            whole, unit_of = coded(value)
            coded_blocks[b] = whole
            scales[b] = jnp.broadcast_to(unit_of, (R, BS))
        for d in range(W):
            spread = jnp.zeros((R, BS), jnp.float32)
            for c in range(C):
                value = coded_blocks[local[d * C + c]]
                (rb if d == 0 else sb)[pl.ds((d * C + c) * R, R), :] = value
                spread = jnp.where(lane == c, scales[local[d * C + c]], spread)
            (rs1 if d == 0 else ss)[pl.ds(d * R, R), :] = spread
            if d:
                request(d).start()
                request_scale(d).start()

        def group(d, carry):
            @pl.when(d > 0)
            def _():
                request(d).wait_recv()
                request_scale(d).wait_recv()

            scale_rows = pl.ds(pl.multiple_of(d * R, R), R)
            scale = rs1[scale_rows, :]
            spread = jnp.zeros((R, BS), jnp.float32)
            for c in range(C):
                p = d * C + c
                rows = pl.ds(pl.multiple_of(p * R, R), R)
                tile = tiles[p]
                high, low = split(number(rb[rows, :]))
                left = jnp.concatenate(
                    [
                        jnp.concatenate([high, high], axis=1),
                        jnp.concatenate([low, jnp.zeros_like(low)], axis=1),
                    ],
                    axis=0,
                )
                both = dot_nt(left, tile)
                tf[rows, :] = (both[:R] + both[R:]) * scale[:, c : c + 1]
                high, low = split(blocks[first[p]])
                both = jnp.dot(
                    jnp.concatenate([high, low], axis=0), tile, preferred_element_type=jnp.float32
                )
                whole, unit_of = coded(both[:R, :BS] + both[R:, :BS] + both[:R, BS:])
                sb2[rows, :] = whole
                spread = jnp.where(lane == c, unit_of, spread)
            ss2[scale_rows, :] = spread

            @pl.when(d > 0)
            def _():
                answer(d).start()
                answer_scale(d).start()

            return carry

        lax.fori_loop(0, W, group, 0)
        for d in range(W):
            if d:
                answer(d).wait_recv()
                answer_scale(d).wait_recv()
            scale = (rs2 if d else ss2)[pl.ds(d * R, R), :]
            for c in range(C):
                rows = pl.ds((d * C + c) * R, R)
                rb2[rows, :] = number((rq if d else sb2)[rows, :]) * scale[:, c : c + 1]

        one_hot = owners[...]
        for n in range(1, N + 1):
            part = lax.rem(nar + n, N)
            spread = jnp.zeros((8, BS), jnp.float32)
            for q in range(RN):
                r = part * RN + q
                x = jnp.concatenate(
                    [tf[pl.ds(r, W * C, stride=R), :], rb2[pl.ds(r, W * C, stride=R), :]], axis=0
                )
                high, low = split(x)
                value = jnp.dot(
                    one_hot,
                    jnp.concatenate([high, low], axis=0),
                    preferred_element_type=jnp.float32,
                )
                if n == N:
                    acc[pl.ds(q * B, B), :] = value
                else:
                    whole, unit_of = coded(value, (0, 1))
                    pb[pl.ds(pl.multiple_of(part * PR + q * B, B), B), :] = whole
                    spread = jnp.where(lane8 == q, unit_of, spread)
            if n < N:
                psc[n] = spread
                scatter(n).start()
                scatter_scale(n).start()
        for d in range(1, N):
            scatter(d).wait_recv()
            scatter_scale(d).wait_recv()
        spread = jnp.zeros((8, BS), jnp.float32)
        for q in range(RN):
            rows = pl.ds(q * B, B)
            value = acc[rows, :]
            for d in range(1, N):
                value += number(rs[d, rows, :]) * rsc[d][:1, q : q + 1]
            whole, unit_of = coded(value, (0, 1))
            out16[rows, :] = whole
            all16[pl.ds(pl.multiple_of(nar * PR + q * B, B), B), :] = whole
            spread = jnp.where(lane8 == q, unit_of, spread)
        osc[...] = spread
        asc[nar] = spread
        for d in range(1, N):
            gather(d).start()
            gather_scale(d, nar).start()
        for d in range(1, N):
            gathered(d).wait_recv()
            gather_scale(d, lax.rem(nar - d + N, N)).wait_recv()
        for r in range(R):
            rows = pl.ds(r * B, B)
            unit_of = asc[r // RN][:1, r % RN : r % RN + 1]
            ag[rows, :] = number(all16[rows, :]) * unit_of

        for b in range(B):
            xs[R:, b * BS : (b + 1) * BS] = ag[pl.ds(b, R, stride=B), :]
        xs[R:, :] = xs[R:, :] - dot32(up[...], prev[...])
        summed = gram_sum(dot_nt(xs[...], xs[...], HIGH))
        basis_gram = summed[:R, :R]
        along = summed[:R, R:]
        along_t = summed[R:, :R]
        raw = summed[R:, R:]
        gram = raw - 2.0 * dot32(along_t, along) + dot32(along_t, dot32(basis_gram, along))
        lower, upper, inverse = factor_of(gram, R)
        coef[k, 0] = along
        coef[k, 1] = lower
        prev[...] = xs[:R, :]
        up[...] = upper
        mix = jnp.concatenate([-dot32(inverse, along_t), inverse], axis=1)
        xs[:R, :] = dot32(mix, xs[...])

        for d in range(1, W):
            request(d).wait_send()
            answer(d).wait_send()
            request_scale(d).wait_send()
            answer_scale(d).wait_send()
        for d in range(1, N):
            scatter(d).wait_send()
            gather(d).wait_send()
            scatter_scale(d).wait_send()
            gather_scale(d, nar).wait_send()
        return carry

    lax.fori_loop(0, STEPS, step, 0)
    out[...] = xs[:R, :]


def quarter_scale(code):
    return jnp.exp(code.astype(jnp.float32) * (1.0 / LOG_STEPS))


def packed(values):
    top = jnp.abs(values[0])
    for value in values[1:]:
        top = jnp.maximum(top, jnp.abs(value))
    top = jnp.maximum(jnp.max(top, axis=1, keepdims=True), 1e-30)
    whole = jnp.ceil(jnp.log(top) * LOG_STEPS).astype(jnp.int32)
    whole = jnp.broadcast_to(whole, values[0].shape)
    factor = LEVELS / quarter_scale(whole)
    out = [
        jnp.clip(jnp.round(value * factor), -LEVELS, LEVELS).astype(jnp.int32).astype(jnp.int16)
        for value in values
    ]
    return out + [whole.astype(jnp.int16)]


SLOTS = 5
Z_ROWS = 48
PARTS = 4


def fused_kernel(dims, names, points, q_ref, pairs_ref, out, coef, *refs):
    W, N, C, R, B, F, total = dims
    s_ = dict(zip(names, refs))
    (unit, uq0, uq1, uq2, uq3, uq4, kt, tf1, tf2, vo, vr, rep, perm, shift, yt, zt, oht1, oht2, oh1, oh2, lv, ls, idx_i, idx_j, n2, w2, o1n, o1w, i1n, i1w,
     y1, y2, gs, gn, gt, gw, fin, qc, pv, wp, zp, at, inv, up) = (s_[n] for n in DATA)
    sem = s_
    uq = (uq0, uq1, uq2, uq3, uq4)
    QR = BS // N
    JQ = B // N
    HALF = W * C
    me = lax.axis_index("wide")
    nar = lax.axis_index("narrow")
    z, x = lax.div(me, 2), lax.rem(me, 2)
    h = lax.div(z, 2)
    e = lax.rem(z, 2)
    cd = (1 - h) * (3 - z) + h * (z - 2)
    cs = (1 - h) * (z + 2) + h * (3 - z)
    ax = 1 - x
    side = z + 1 - 2 * e
    XN = 2 * z + ax
    SRC = [XN, 2 * cs + x, 2 * cs + ax, 2 * side + (1 - e) * ax + e * x]
    DST = [XN, 2 * cd + x, 2 * cd + ax, 2 * side + (1 - e) * x + e * ax]
    GROUP = [me] + SRC
    lane = lax.broadcasted_iota(jnp.int32, (R, BS), 1)
    lane8 = lax.broadcasted_iota(jnp.int32, (8, BS), 1)
    sub8 = lax.broadcasted_iota(jnp.int32, (8, BS), 0)

    def slot_is(s, lanes=None):
        lanes = lane if lanes is None else lanes
        return (lanes >= s * QR) & (lanes < s * QR + QR)

    def filled(value):
        value = value + pltpu.roll(value, QR, 1)
        return value + pltpu.roll(value, 2 * QR, 1)

    def remote(src, dst, name, at_, where):
        return pltpu.make_async_remote_copy(
            src_ref=src, dst_ref=dst, send_sem=sem["s_" + name].at[at_], recv_sem=sem["r_" + name].at[at_],
            device_id=where, device_id_type=MESH,
        )

    def wide(d):
        return {"wide": d}

    def nearby(d):
        return {"narrow": lax.rem(nar + d, N)}

    def behind(d):
        return lax.rem(nar - d + N, N)

    PART = B // PARTS

    def part(s, t):
        return uq[s].at[pl.ds(t * PART, PART)]

    def hop_x(t):
        return remote(part(0, t), part(1, t), "px", t, wide(XN))

    def hop_c(t):
        return remote(part(0, t), part(2, t), "pc", t, wide(DST[1]))

    def hop_f(t):
        return remote(part(2, t), part(3, t), "pf", t, wide(XN))

    def hop_a(t, s=0):
        return remote(part(s, t), part(4, t), "pa", t, wide(2 * side + x))

    def list_near(d):
        return remote(pairs_ref, lv.at[0, nar], "ln", d, nearby(d))

    def list_wide(d):
        return remote(lv.at[0], lv.at[d], "lw", d, wide(DST[d]))

    def vec_near(k, d):
        return remote(n2.at[k, nar], n2.at[k, nar], "vn", (k, d), nearby(d))

    def vec_near_in(k, d):
        place = n2.at[k, behind(d)]
        return remote(place, place, "vn", (k, d), nearby(d))

    def vec_wide(k, d):
        return remote(n2.at[k, nar], w2.at[k, d], "vw", (k, d), wide(DST[d]))

    def sum_near(k, d):
        return remote(o1n.at[k, d], i1n.at[k, d], "sn", (k, d), nearby(d))

    def sum_wide(k, d):
        return remote(o1w.at[k, d], i1w.at[k, d], "sw", (k, d), wide(SRC[d]))

    def gram_near(k, d):
        return remote(gs.at[k], gn.at[k, nar], "gn", (k, d), nearby(d))

    def gram_near_in(k, d):
        place = gn.at[k, behind(d)]
        return remote(place, place, "gn", (k, d), nearby(d))

    def gram_wide(k, d):
        return remote(gt.at[k], gw.at[k, me], "gw", (k, d), wide(lax.rem(me + d, W)))

    def gram_wide_in(k, d):
        place = gw.at[k, lax.rem(me - d + W, W)]
        return remote(place, place, "gw", (k, d), wide(lax.rem(me + d, W)))

    def fin_near(d):
        return remote(fin.at[nar], fin.at[nar], "fn", d, nearby(d))

    def fin_near_in(d):
        place = fin.at[behind(d)]
        return remote(place, place, "fn", d, nearby(d))

    barrier = pltpu.get_barrier_semaphore()
    for d in range(1, W):
        pl.semaphore_signal(barrier, inc=1, device_id=wide(lax.rem(me + d, W)), device_id_type=MESH)
    for d in range(1, N):
        pl.semaphore_signal(barrier, inc=1, device_id=nearby(d), device_id_type=MESH)

    def normalise(b, carry):
        unit[b] = unit_rows(points[pl.ds(pl.multiple_of(b * BS, BS), BS), :])
        return carry

    def quarter(b, carry):
        uq0[b] = unit_rows(points[pl.ds(pl.multiple_of(b * BS + nar * QR, QR), QR), :])
        return carry

    lax.fori_loop(0, B, quarter, 0, unroll=4)

    def square(x_):
        four = jnp.concatenate([x_] * (BS // (2 * R)), axis=0)
        full = dot_nt(x_, four, HIGH)
        small = jnp.zeros((8, BS), jnp.float32)
        for a in range(2 * R // 8):
            small = jnp.where(slot_is(a, lane8), full[8 * a : 8 * a + 8], small)
        return small

    def gram_value(k):
        total_ = gw[k, 0]
        for d in range(1, W):
            total_ = total_ + gw[k, d]
        rows = [total_] + [pltpu.roll(total_, BS - a * 2 * R, 1) for a in range(1, 2 * R // 8)]
        return jnp.concatenate(rows, axis=0)[:, : 2 * R] / total

    def gram_send(k):
        gw[k, me] = gt[k]
        for d in range(1, W):
            gram_wide(k, d).start()

    def gram_collect(k):
        for d in range(1, N):
            gram_near_in(k, d).wait_recv()
        value = gn[k, 0]
        for d in range(1, N):
            value = value + gn[k, d]
        gt[k] = value
        gram_send(k)

    def gram_start(k):
        value = square(jnp.concatenate([qc[...], wp[...]], axis=0))
        gs[k] = value
        gn[k, nar] = value
        for d in range(1, N):
            gram_near(k, d).start()

    def gram_finish(k):
        for d in range(1, W):
            gram_wide_in(k, d).wait_recv()
        summed = gram_value(k)
        along = summed[:R, R:]
        along_t = summed[R:, :R]
        gram = summed[R:, R:] - 2.0 * dot32(along_t, along) + dot32(along_t, dot32(summed[:R, :R], along))
        lower, upper, inverse = factor_of(gram, R)
        coef[k - 1, 0] = along
        coef[k - 1, 1] = lower
        at[...] = along_t
        inv[...] = inverse
        up[...] = upper
        pv[...] = qc[...]
        qc[...] = dot32(inverse, wp[...] - dot32(along_t, qc[...]))

    lv[0, nar] = pairs_ref[...]
    q_all = q_ref[...]
    gt[0] = square(jnp.concatenate([q_all, q_all], axis=0))
    pl.semaphore_wait(barrier, W - 1 + N - 1)

    for d in range(1, N):
        list_near(d).start()
    gram_send(0)
    hop_c(0).start()
    hop_x(0).start()
    for d in range(1, N):
        place = lv.at[0, behind(d)]
        remote(place, place, "ln", d, nearby(d)).wait_recv()
    for d in range(1, 4):
        list_wide(d).start()
    for t in range(1, PARTS):
        hop_c(t).start()
        hop_x(t).start()

    @pl.when(e == 0)
    def _():
        for t in range(PARTS):
            hop_a(t).start()

    def relay_x(t):
        hop_x(t).wait_recv()

        @pl.when(e == 1)
        def _():
            hop_a(t, 1).start()

    def relay_c(t):
        hop_c(t).wait_recv()
        hop_f(t).start()

    lax.fori_loop(0, B, normalise, 0, unroll=2)

    def places(rows, columns, of):
        row = lax.broadcasted_iota(jnp.int32, (rows, columns), 0)
        column = lax.broadcasted_iota(jnp.int32, (rows, columns), 1)
        return (row == of(column)).astype(jnp.float32).astype(jnp.bfloat16)

    rep[...] = places(BS, N * BS, lambda l: (l // BS) * QR + (l & (QR - 1)))
    perm[...] = places(
        N * BS, N * BS, lambda l: ((l // QR) & (N - 1)) * BS + (l // BS) * QR + (l & (QR - 1))
    )
    for a in range(N):
        shift[a * BS : (a + 1) * BS, :] = places(
            BS, BS, lambda l: ((l // QR + N - a) & (N - 1)) * QR + (l & (QR - 1))
        )

    relay_x(0)
    for jq in range(JQ):
        value = jnp.zeros((R, BS), jnp.float32)
        for s in range(N):
            b = N * jq + s
            one = filled(jnp.where(slot_is(nar), q_ref[:, b * BS : (b + 1) * BS], 0.0))
            value = jnp.where(slot_is(s), one, value)
        wp[:, jq * BS : (jq + 1) * BS] = value

    relay_x(1)
    relay_c(0)
    for d in range(1, W):
        gram_wide_in(0, d).wait_recv()
    _, _, inverse0 = factor_of(gram_value(0)[:R, :R], R)
    qc[...] = dot32(inverse0, wp[...])
    for ref in (pv, zp, at, up):
        ref[...] = jnp.zeros_like(ref)
    inv[...] = (
        lax.broadcasted_iota(jnp.int32, (R, R), 0) == lax.broadcasted_iota(jnp.int32, (R, R), 1)
    ).astype(jnp.float32)

    def lanes_of(ref):
        return [ref[:, jq * BS : (jq + 1) * BS] for jq in range(JQ)]

    def vec_send(k, ref):
        for jq, value in enumerate(packed(lanes_of(ref))):
            n2[k, nar, jq * R : (jq + 1) * R, :] = value
        for d in range(1, N):
            vec_near(k, d).start()
        for d in range(4):
            vec_wide(k, d).start()

    vec_send(0, qc)
    relay_x(2)
    for d in range(1, 4):
        remote(lv.at[d], lv.at[d], "lw", d, wide(DST[d])).wait_recv()
    local = pltpu.make_async_copy(lv, ls, sem["m_ls"])
    local.start()
    local.wait()

    kinds = []
    for s in range(SLOTS):
        kinds.append((s, 0))
        if s > 1:
            kinds.append((s, 1))

    for at_kind, (s, kind) in enumerate(kinds):
        other = GROUP[s]

        def indices(mq, carry):
            ch = at_kind * N + mq
            vi = jnp.zeros((8, BS), jnp.int32)
            vj = jnp.zeros((8, BS), jnp.int32)
            for c in range(C):
                if kind == 0:
                    i = lax.rem(ls[0, mq, 0, other * C + c], B)
                    j = lax.rem(ls[0, mq, 0, HALF + other * C + c], B)
                else:
                    j = lax.rem(ls[s - 1, mq, 0, me * C + c], B)
                    i = lax.rem(ls[s - 1, mq, 0, HALF + me * C + c], B)
                idx_i[ch * C + c] = i
                idx_j[ch * C + c] = j
                vi = jnp.where(sub8 == c, i, vi)
                vj = jnp.where(sub8 == c, j, vj)
            rows = pl.ds(pl.multiple_of(ch * C, C), C)
            row = (vi & (N - 1)) * JQ + vi // N
            oht1[rows, :] = (row == lane8).astype(jnp.float32)
            row = ((vj + N - (sub8 & (N - 1))) & (N - 1)) * Z_ROWS + s * JQ + vj // N
            oht2[rows, :BS] = (row == lane8).astype(jnp.float32)
            oht2[rows, BS:] = (row == lane8 + BS).astype(jnp.float32)
            return carry

        lax.fori_loop(0, N, indices, 0)

    relay_x(3)
    relay_c(1)
    turned = jnp.transpose(oht1[...])[: oh1.shape[0]].astype(jnp.bfloat16)
    oh1[...] = jnp.concatenate([turned, turned], axis=1)
    turned = jnp.transpose(oht2[...])[: oh2.shape[0]].astype(jnp.bfloat16)
    oh2[...] = jnp.concatenate([turned, turned], axis=1)

    def tiles_of(want):
        for at_kind, (s, kind) in enumerate(kinds):
            if s != want:
                continue

            def make(mq, carry):
                ch = at_kind * N + mq
                for c in range(C):
                    p = ch * C + c
                    sim = dot_nt(uq[s][idx_j[p]], unit[idx_i[p]])
                    high, low = split(jnp.exp(KERNEL_FACTOR * (sim - 1.0)))
                    rows = pl.ds(pl.multiple_of(p * QR, QR), QR)
                    kt[rows, :BS] = high
                    kt[rows, BS:] = low
                return carry

            lax.fori_loop(0, N, make, 0)

    tiles_of(0)
    relay_c(2)
    tiles_of(1)
    relay_c(3)
    tiles_of(2)
    for t in range(PARTS):
        hop_a(t).wait_recv()
    tiles_of(4)
    for t in range(PARTS):
        hop_f(t).wait_recv()
    tiles_of(3)

    chunks = len(kinds) * N
    slots_of_chunk = [s for s, _ in kinds for _ in range(N)]

    def unpacked(ref, k, d):
        scale = quarter_scale(ref[k, d, JQ * R : (JQ + 1) * R, :].astype(jnp.int32)) * (1.0 / LEVELS)
        return [number(ref[k, d, jq * R : (jq + 1) * R, :]) * scale for jq in range(JQ)]

    def both(value):
        return jnp.concatenate(split(value), axis=0)

    def scatter(tf, one_hot, keep):
        for r in range(0, R, 2):
            columns = []
            for q in range(2):
                high, low = split(tf[pl.ds(r + q, chunks * C, stride=R), :])
                columns.append(jnp.concatenate([high, low], axis=0))
            value = jnp.dot(
                one_hot[...], jnp.concatenate(columns, axis=1), preferred_element_type=jnp.float32
            )
            keep(r, value[:, :BS])
            keep(r + 1, value[:, BS:])

    def moved(value, matrix):
        rows = value.shape[0]
        value = jnp.dot(both(value), matrix[...], preferred_element_type=jnp.float32)
        return value[:rows] + value[rows:]

    def step(k, carry):
        for d in range(1, N):
            vec_near_in(k, d).wait_recv()
        quarters = [unpacked(n2, k, q) for q in range(N)]
        pieces = [
            jnp.concatenate([both(quarters[q][jq]) for q in range(N)], axis=1) for jq in range(JQ)
        ]
        value = jnp.dot(jnp.concatenate(pieces, axis=0), perm[...], preferred_element_type=jnp.float32)
        value = value.astype(jnp.bfloat16)
        for jq in range(JQ):
            for s in range(N):
                vo[jq * N + s] = value[2 * R * jq : 2 * R * (jq + 1), s * BS : (s + 1) * BS]
        mine = unpacked(n2, k, nar)

        def keep_remote(s, values):
            value = jnp.dot(
                jnp.concatenate([both(v) for v in values], axis=0), rep[...],
                preferred_element_type=jnp.float32,
            ).astype(jnp.bfloat16)
            for jq in range(JQ):
                for b in range(N):
                    vr[s * B + jq * N + b] = value[2 * R * jq : 2 * R * (jq + 1), b * BS : (b + 1) * BS]

        keep_remote(0, mine)

        @pl.when(k > 0)
        def _():
            gram_collect(k)

        def second(ch, carry):
            left = jnp.concatenate([vo[idx_i[ch * C + c]] for c in range(C)], axis=0)
            tile = kt[pl.ds(pl.multiple_of(ch * C * QR, C * QR), C * QR), :]
            full = dot_nt(jnp.concatenate([left, left], axis=1), tile)
            for c in range(C):
                columns = slice((c // N) * BS, (c // N + 1) * BS)
                value = full[2 * R * c : 2 * R * c + R, columns] + full[2 * R * c + R : 2 * R * (c + 1), columns]
                value = jnp.where(slot_is(c % N), value, 0.0)
                tf2[pl.ds(pl.multiple_of((ch * C + c) * R, R), R), :] = value
            return carry

        lax.fori_loop(0, chunks, second, 0, unroll=4)

        def keep2(r, value):
            for a in range(N):
                zt[r * SLOTS * JQ : (r + 1) * SLOTS * JQ, a * BS : (a + 1) * BS] = (
                    value[a * Z_ROWS : a * Z_ROWS + SLOTS * JQ]
                )

        scatter(tf2, oh2, keep2)
        batch = R // 4
        for first_r in range(0, R, batch):
            value = moved(zt[first_r * SLOTS * JQ : (first_r + batch) * SLOTS * JQ, :], shift)
            for r in range(batch):
                for s in range(SLOTS):
                    place = (r * SLOTS + s) * JQ
                    y2[s, pl.ds(first_r + r, JQ, stride=R), :] = value[place : place + JQ]
        for d in range(4):
            for jq, value in enumerate(packed([y2[d + 1, jq * R : (jq + 1) * R, :] for jq in range(JQ)])):
                o1w[k, d, jq * R : (jq + 1) * R, :] = value
            sum_wide(k, d).start()

        for d in range(4):
            remote(w2.at[k, d], w2.at[k, d], "vw", (k, d), wide(DST[d])).wait_recv()
            keep_remote(d + 1, unpacked(w2, k, d))

        for s in range(SLOTS):
            first_chunk = slots_of_chunk.index(s)

            def first(ch, carry):
                left = []
                for c in range(C):
                    value = vr[s * B + idx_j[ch * C + c]]
                    value = jnp.where(slot_is(c % N, lane2), value, jnp.zeros_like(value))
                    pieces = [jnp.zeros_like(value)] * (C // N)
                    pieces[c // N] = value
                    left.append(jnp.concatenate(pieces, axis=1))
                tile = kt[pl.ds(pl.multiple_of(ch * C * QR, C * QR), C * QR), :]
                full = jnp.dot(jnp.concatenate(left, axis=0), tile, preferred_element_type=jnp.float32)
                for c in range(C):
                    high = full[2 * R * c : 2 * R * c + R]
                    low = full[2 * R * c + R : 2 * R * (c + 1)]
                    tf1[pl.ds(pl.multiple_of((ch * C + c) * R, R), R), :] = (
                        high[:, :BS] + high[:, BS:] + low[:, :BS]
                    )
                return carry

            lax.fori_loop(first_chunk, first_chunk + slots_of_chunk.count(s), first, 0, unroll=4)

        def keep1(r, value):
            for s in range(N):
                yt[r * JQ : (r + 1) * JQ, s * BS : (s + 1) * BS] = value[s * JQ : (s + 1) * JQ]

        scatter(tf1, oh1, keep1)
        value = moved(yt[...], perm)
        for r in range(R):
            for q in range(N):
                y1[q, pl.ds(r, JQ, stride=R), :] = value[r * JQ : (r + 1) * JQ, q * BS : (q + 1) * BS]

        for d in range(1, N):
            to = lax.rem(nar + d, N)
            for jq, value in enumerate(packed([y1[to, jq * R : (jq + 1) * R, :] for jq in range(JQ)])):
                o1n[k, d, jq * R : (jq + 1) * R, :] = value
            sum_near(k, d).start()

        @pl.when(k > 0)
        def _():
            gram_finish(k)

        image = [y1[nar, jq * R : (jq + 1) * R, :] + y2[0, jq * R : (jq + 1) * R, :] for jq in range(JQ)]
        for d in range(4):
            sum_wide(k, d).wait_recv()
            image = [a + b for a, b in zip(image, unpacked(i1w, k, d))]
        for d in range(1, N):
            sum_near(k, d).wait_recv()
            image = [a + b for a, b in zip(image, unpacked(i1n, k, d))]
        image = jnp.concatenate(image, axis=1)
        image = dot32(inv[...], image - dot32(at[...], zp[...]))
        zp[...] = image
        wp[...] = image - dot32(up[...], pv[...])

        @pl.when(k < STEPS - 1)
        def _():
            vec_send(k + 1, wp)

        gram_start(k + 1)
        return carry

    lane2 = lax.broadcasted_iota(jnp.int32, (2 * R, BS), 1)
    lax.fori_loop(0, STEPS, step, 0)
    gram_collect(STEPS)
    gram_finish(STEPS)
    for jq, value in enumerate(lanes_of(qc)):
        fin[nar, jq * R : (jq + 1) * R, :] = value
    for d in range(1, N):
        fin_near(d).start()
    for d in range(1, N):
        fin_near_in(d).wait_recv()
    value = moved(jnp.concatenate([fin[q] for q in range(N)], axis=1), perm)
    for jq in range(JQ):
        for s in range(N):
            b = jq * N + s
            out[:, b * BS : (b + 1) * BS] = value[jq * R : (jq + 1) * R, s * BS : (s + 1) * BS]

    for t in range(PARTS):
        hop_x(t).wait_send()
        hop_c(t).wait_send()
        hop_a(t).wait_send()
        hop_f(t).wait_send()
    for d in range(1, N):
        list_near(d).wait_send()
        fin_near(d).wait_send()
    for d in range(1, 4):
        list_wide(d).wait_send()
    for d in range(1, W):
        gram_wide(0, d).wait_send()
    for k in range(STEPS):
        for d in range(1, N):
            vec_near(k, d).wait_send()
            sum_near(k, d).wait_send()
            gram_near(k + 1, d).wait_send()
        for d in range(4):
            vec_wide(k, d).wait_send()
            sum_wide(k, d).wait_send()
        for d in range(1, W):
            gram_wide(k + 1, d).wait_send()


DATA = (
    "unit", "uq0", "uq1", "uq2", "uq3", "uq4", "kt", "tf1", "tf2", "vo", "vr", "rep", "perm", "shift", "yt", "zt", "oht1", "oht2",
    "oh1", "oh2", "lv", "ls", "idx_i", "idx_j", "n2", "w2", "o1n", "o1w", "i1n", "i1w", "y1", "y2",
    "gs", "gn", "gt", "gw", "fin", "qc", "pv", "wp", "zp", "at", "inv", "up",
)


def fused(points, q_init, pairs, W, N):
    R, cols = q_init.shape
    F = points.shape[1]
    B = cols // BS
    pair_count = pairs.shape[1]
    C = pair_count // W
    QR, JQ = BS // N, B // N
    P_ = (SLOTS + SLOTS - 2) * N * C
    f32, bf16, i16, i32 = jnp.float32, jnp.bfloat16, jnp.int16, jnp.int32
    V = pltpu.VMEM
    message = ((JQ + 1) * R, BS)
    rounds = STEPS + 1
    columns = JQ * BS
    shapes = {
        "unit": V((B, BS, F), bf16), **{f"uq{s}": V((B, QR, F), bf16) for s in range(SLOTS)}, "kt": V((P_ * QR, 2 * BS), bf16),
        "tf1": V((P_ * R, BS), f32), "tf2": V((P_ * R, BS), f32),
        "vo": V((B, 2 * R, BS), bf16), "vr": V((SLOTS * B, 2 * R, BS), bf16),
        "oht1": V((P_, BS), f32), "oht2": V((P_, 2 * BS), f32),
        "rep": V((BS, N * BS), bf16), "perm": V((N * BS, N * BS), bf16), "shift": V((N * BS, BS), bf16),
        "yt": V((R * JQ, N * BS), f32), "zt": V((R * SLOTS * JQ, N * BS), f32),
        "oh1": V((B, 2 * P_), bf16), "oh2": V((N * Z_ROWS, 2 * P_), bf16),
        "lv": V((4, N, 1, 2 * pair_count), i32), "ls": pltpu.SMEM((4, N, 1, 2 * pair_count), i32),
        "idx_i": pltpu.SMEM((P_,), i32), "idx_j": pltpu.SMEM((P_,), i32),
        "n2": V((STEPS, N) + message, i16), "w2": V((STEPS, 4) + message, i16),
        "o1n": V((STEPS, N) + message, i16), "o1w": V((STEPS, 4) + message, i16),
        "i1n": V((STEPS, N) + message, i16), "i1w": V((STEPS, 4) + message, i16),
        "y1": V((N, JQ * R, BS), f32), "y2": V((SLOTS, JQ * R, BS), f32),
        "gs": V((rounds, 8, BS), f32), "gn": V((rounds, N, 8, BS), f32),
        "gt": V((rounds, 8, BS), f32), "gw": V((rounds, W, 8, BS), f32),
        "fin": V((N, JQ * R, BS), f32),
        "qc": V((R, columns), f32), "pv": V((R, columns), f32), "wp": V((R, columns), f32),
        "zp": V((R, columns), f32),
        "at": V((R, R), f32), "inv": V((R, R), f32), "up": V((R, R), f32),
    }
    sems = {
        "px": (PARTS,), "pc": (PARTS,), "pf": (PARTS,), "pa": (PARTS,), "ln": (N,), "lw": (4,),
        "vn": (STEPS, N), "vw": (STEPS, 4), "sn": (STEPS, N), "sw": (STEPS, 4),
        "gn": (rounds, N), "gw": (rounds, W), "fn": (N,),
    }
    names = list(DATA)
    scratch = [shapes[n] for n in DATA]
    for name, shape in sems.items():
        for way in "sr":
            names.append(way + "_" + name)
            scratch.append(pltpu.SemaphoreType.DMA(shape))
    names.append("m_ls")
    scratch.append(pltpu.SemaphoreType.DMA)
    vmem = pl.BlockSpec(memory_space=pltpu.VMEM)
    dims = (W, N, C, R, B, F, B * BS * W)
    return pl.pallas_call(
        functools.partial(fused_kernel, dims, tuple(names)),
        out_shape=(
            jax.ShapeDtypeStruct((R, cols), f32),
            jax.ShapeDtypeStruct((STEPS, 2, R, R), f32),
        ),
        in_specs=[vmem, vmem, vmem],
        out_specs=(vmem, vmem),
        scratch_shapes=scratch,
        compiler_params=pltpu.CompilerParams(collective_id=1, has_side_effects=True),
        name="fused",
    )(points, q_init, pairs.reshape(1, 2 * pair_count))


def lanczos(first, local, owners, tiles, q_init, wide_count, narrow_count, total):
    R, cols = q_init.shape
    B = cols // BS
    pair_count = first.shape[0]
    C = pair_count // wide_count
    dims = (wide_count, narrow_count, C, R, B, total)
    vmem = pl.BlockSpec(memory_space=pltpu.VMEM)
    smem = pl.BlockSpec(memory_space=pltpu.SMEM)
    f32 = jnp.float32
    pairs_buf = pltpu.VMEM((pair_count * R, BS), f32)
    coded_buf = pltpu.VMEM((pair_count * R, BS), jnp.int16)
    scale_buf = pltpu.VMEM((wide_count * R, BS), f32)
    part = R // narrow_count * B
    wide_sem = pltpu.SemaphoreType.DMA((wide_count,))
    narrow_sem = pltpu.SemaphoreType.DMA((narrow_count,))
    return pl.pallas_call(
        functools.partial(main_kernel, dims),
        out_shape=(
            jax.ShapeDtypeStruct((R, cols), f32),
            jax.ShapeDtypeStruct((STEPS, 2, R, R), f32),
        ),
        in_specs=[smem, smem, vmem, vmem, vmem],
        out_specs=(vmem, vmem),
        scratch_shapes=[
            coded_buf, coded_buf, coded_buf, coded_buf,
            scale_buf, scale_buf, scale_buf, scale_buf,
            pltpu.VMEM((B, R, BS), jnp.int16),
            pltpu.VMEM((B, R, BS), f32),
            pairs_buf, pairs_buf,
            pltpu.VMEM((R * B, BS), jnp.int16),
            pltpu.VMEM((narrow_count, part, BS), jnp.int16),
            pltpu.VMEM((R * B, BS), f32),
            pltpu.VMEM((part, BS), f32),
            pltpu.VMEM((part, BS), jnp.int16),
            pltpu.VMEM((R * B, BS), jnp.int16),
            pltpu.VMEM((narrow_count, 8, BS), f32),
            pltpu.VMEM((narrow_count, 8, BS), f32),
            pltpu.VMEM((8, BS), f32),
            pltpu.VMEM((narrow_count, 8, BS), f32),
            pltpu.VMEM((2 * R, cols), f32),
            pltpu.VMEM((B, R, BS), f32),
            pltpu.VMEM((R, cols), f32),
            pltpu.VMEM((R, R), f32),
            pltpu.VMEM((2 * R, BS), f32),
            pltpu.VMEM((wide_count, 2 * R, BS), f32),
            wide_sem, wide_sem, wide_sem, wide_sem,
            narrow_sem, narrow_sem, narrow_sem, narrow_sem,
            wide_sem, wide_sem, wide_sem, wide_sem, wide_sem, wide_sem,
            narrow_sem, narrow_sem, narrow_sem, narrow_sem,
        ],
        compiler_params=pltpu.CompilerParams(collective_id=0, has_side_effects=True),
        name="lanczos",
    )(first, local, owners, tiles, q_init)


def per_device(points, q_init, pairs):
    wide_count = lax.axis_size("wide")
    narrow_count = lax.axis_size("narrow")
    me = lax.axis_index("wide")
    own_blocks = points.shape[0] // BS
    width = points.shape[1]
    pair_count = pairs.shape[1]
    capacity = pair_count // wide_count
    if wide_count == 8 and narrow_count == 4 and own_blocks == 8 * narrow_count and capacity == 8:
        return fused(points, q_init, pairs, wide_count, narrow_count)
    total = own_blocks * BS * wide_count
    unit = unit_rows(points).reshape(own_blocks, BS, width)
    turn = jnp.arange(wide_count, dtype=jnp.int32)
    first_rows = (pairs[0] - me * own_blocks).reshape(wide_count, capacity)
    first = first_rows[(me - turn) % wide_count].reshape(pair_count)
    second = (pairs[1].reshape(wide_count, capacity) - turn[:, None] * own_blocks)
    every = lax.all_to_all(
        jnp.broadcast_to(second.reshape(1, pair_count), (wide_count, pair_count)),
        "wide", split_axis=0, concat_axis=0, tiled=True,
    ).reshape(wide_count, wide_count, capacity)
    local_ids = lax.dynamic_index_in_dim(every, me, axis=1, keepdims=False)
    local = local_ids[(me + turn) % wide_count].reshape(pair_count)
    targets = jnp.concatenate([first, local, first, local])
    owners = (jnp.arange(own_blocks, dtype=jnp.int32)[:, None] == targets[None, :]).astype(
        jnp.bfloat16
    )
    blocks = lax.all_to_all(
        unit[local_ids.reshape(pair_count)], "wide", split_axis=0, concat_axis=0, tiled=True
    ).reshape(wide_count, capacity, BS, width)
    tiles = make_tiles(jnp.reshape(me, (1,)).astype(jnp.int32), first, unit, blocks)
    return lanczos(first, local, owners, tiles, q_init, wide_count, narrow_count, total)


def solution(mesh):
    placed = (P("wide", None), P(None, "wide"), P(None, ("wide", "narrow")))
    return jax.shard_map(
        per_device, mesh=mesh, in_specs=placed, out_specs=(P(None, "wide"), P()), check_vma=False
    )
```

```python
import functools

import jax
import jax.numpy as jnp
from jax import lax
from jax.experimental import pallas as pl
from jax.experimental.pallas import tpu as pltpu
from jax.sharding import PartitionSpec as P

BS = 128
STEPS = 3
LEVELS = 32767.0
KERNEL_FACTOR = 3.0
EPSILON = 1e-06
LOG_STEPS = 256.0
HIGH = lax.Precision.HIGHEST
MESH = pl.DeviceIdType.MESH


def unit_rows(points):
    wide32 = points.astype(jnp.float32)
    scaled = wide32 * lax.rsqrt(jnp.sum(wide32 * wide32, axis=-1, keepdims=True) + EPSILON)
    return scaled.astype(jnp.bfloat16)


def split(x):
    high = x.astype(jnp.bfloat16)
    return high, (x - high.astype(jnp.float32)).astype(jnp.bfloat16)


def coded(x, axes=1):
    top = jnp.maximum(jnp.max(jnp.abs(x), axis=axes, keepdims=True), 1e-30)
    scaled = jnp.clip(jnp.round(x * (LEVELS / top)), -LEVELS, LEVELS)
    return scaled.astype(jnp.int32).astype(jnp.int16), top * (1.0 / LEVELS)


def number(x):
    return x.astype(jnp.int32).astype(jnp.float32)


def dot32(a, b):
    return jnp.dot(a, b, precision=HIGH, preferred_element_type=jnp.float32)


def dot_nt(a, b, precision=None):
    return lax.dot_general(
        a, b, (((1,), (1,)), ((), ())), precision=precision, preferred_element_type=jnp.float32
    )


def tiles_kernel(capacity, me_ref, first_ref, unit_ref, second_ref, out_ref):
    d = pl.program_id(0)
    for c in range(capacity):
        s = dot_nt(unit_ref[first_ref[d * capacity + c]], second_ref[0, c])
        high, low = split(jnp.exp(KERNEL_FACTOR * (s - 1.0)))
        out_ref[c, :, :BS] = high
        out_ref[c, :, BS:] = low


def make_tiles(me, first, unit, second):
    wide_count, capacity, _, width = second.shape
    own_blocks = unit.shape[0]
    spec = pltpu.PrefetchScalarGridSpec(
        num_scalar_prefetch=2,
        grid=(wide_count,),
        in_specs=[
            pl.BlockSpec((own_blocks, BS, width), lambda d, m, f: (0, 0, 0)),
            pl.BlockSpec(
                (1, capacity, BS, width),
                lambda d, m, f: (lax.rem(m[0] - d + wide_count, wide_count), 0, 0, 0),
            ),
        ],
        out_specs=pl.BlockSpec((capacity, BS, 2 * BS), lambda d, m, f: (d, 0, 0)),
    )
    return pl.pallas_call(
        functools.partial(tiles_kernel, capacity),
        grid_spec=spec,
        out_shape=jax.ShapeDtypeStruct((wide_count * capacity, BS, 2 * BS), jnp.bfloat16),
        name="tiles",
    )(me, first, unit, second)


def factor_of(gram, r):
    i = lax.broadcasted_iota(jnp.int32, (r, r), 0)
    j = lax.broadcasted_iota(jnp.int32, (r, r), 1)
    both_i = lax.broadcasted_iota(jnp.int32, (r, 2 * r), 0)
    m = jnp.concatenate([gram, (i == j).astype(jnp.float32)], axis=1)
    lower = jnp.zeros((r, r), jnp.float32)
    for k in range(r):
        inv = 1.0 / jnp.sqrt(m[k : k + 1, k : k + 1])
        row = m[k : k + 1, :] * inv
        col = m[:, k : k + 1] * inv
        lower = jnp.where((j == k) & (i >= k), col, lower)
        m = jnp.where(both_i == k, row, jnp.where(both_i > k, m - col * row, m))
    upper = jnp.where(j >= i, m[:, :r], 0.0)
    inverse = jnp.where(j <= i, m[:, r:], 0.0)
    return lower, upper, inverse


def main_kernel(
    dims, first, local, owners, tiles, q_ref, out, coef,
    sb, rb, sb2, rq, ss, rs1, ss2, rs2, coded_blocks, scales, rb2, tf, pb, rs, ag, acc, out16, all16, psc, rsc, osc, asc, xs, blocks, prev, up, gs, gr,
    s1, r1, s2, r2, s3, r3, s4, r4, s5, r5, s6, r6, s7, r7, s8, r8, s9, r9,
):
    W, N, C, R, B, total = dims
    CR = C * R
    RN = R // N
    PR = RN * B
    me = lax.axis_index("wide")
    nar = lax.axis_index("narrow")

    def up_peer(d):
        return lax.rem(me + d, W)

    def down_peer(d):
        return lax.rem(me - d + W, W)

    barrier = pltpu.get_barrier_semaphore()
    for d in range(1, W):
        pl.semaphore_signal(barrier, inc=1, device_id={"wide": up_peer(d)}, device_id_type=MESH)
    for d in range(1, N):
        pl.semaphore_signal(
            barrier, inc=1, device_id={"narrow": lax.rem(nar + d, N)}, device_id_type=MESH
        )
    pl.semaphore_wait(barrier, W - 1 + N - 1)

    def request(d):
        rows = pl.ds(d * CR, CR)
        return pltpu.make_async_remote_copy(
            src_ref=sb.at[rows], dst_ref=rb.at[rows], send_sem=s1.at[d], recv_sem=r1.at[d],
            device_id={"wide": up_peer(d)}, device_id_type=MESH,
        )

    def answer(d):
        rows = pl.ds(d * CR, CR)
        return pltpu.make_async_remote_copy(
            src_ref=sb2.at[rows], dst_ref=rq.at[rows], send_sem=s2.at[d], recv_sem=r2.at[d],
            device_id={"wide": down_peer(d)}, device_id_type=MESH,
        )

    def request_scale(d):
        rows = pl.ds(d * R, R)
        return pltpu.make_async_remote_copy(
            src_ref=ss.at[rows], dst_ref=rs1.at[rows], send_sem=s6.at[d], recv_sem=r6.at[d],
            device_id={"wide": up_peer(d)}, device_id_type=MESH,
        )

    def answer_scale(d):
        rows = pl.ds(d * R, R)
        return pltpu.make_async_remote_copy(
            src_ref=ss2.at[rows], dst_ref=rs2.at[rows], send_sem=s7.at[d], recv_sem=r7.at[d],
            device_id={"wide": down_peer(d)}, device_id_type=MESH,
        )

    lane = lax.broadcasted_iota(jnp.int32, (R, BS), 1)

    def scatter(d):
        return pltpu.make_async_remote_copy(
            src_ref=pb.at[pl.ds(lax.rem(nar + d, N) * PR, PR)], dst_ref=rs.at[d],
            send_sem=s3.at[d], recv_sem=r3.at[d],
            device_id={"narrow": lax.rem(nar + d, N)}, device_id_type=MESH,
        )

    def gather(d):
        mine = pl.ds(nar * PR, PR)
        return pltpu.make_async_remote_copy(
            src_ref=out16, dst_ref=all16.at[mine], send_sem=s4.at[d], recv_sem=r4.at[d],
            device_id={"narrow": lax.rem(nar + d, N)}, device_id_type=MESH,
        )

    def gathered(d):
        theirs = pl.ds(lax.rem(nar - d + N, N) * PR, PR)
        return pltpu.make_async_remote_copy(
            src_ref=out16, dst_ref=all16.at[theirs], send_sem=s4.at[d], recv_sem=r4.at[d],
            device_id={"narrow": lax.rem(nar + d, N)}, device_id_type=MESH,
        )

    def scatter_scale(d):
        return pltpu.make_async_remote_copy(
            src_ref=psc.at[d], dst_ref=rsc.at[d], send_sem=s8.at[d], recv_sem=r8.at[d],
            device_id={"narrow": lax.rem(nar + d, N)}, device_id_type=MESH,
        )

    def gather_scale(d, slot):
        return pltpu.make_async_remote_copy(
            src_ref=osc, dst_ref=asc.at[slot], send_sem=s9.at[d], recv_sem=r9.at[d],
            device_id={"narrow": lax.rem(nar + d, N)}, device_id_type=MESH,
        )

    lane8 = lax.broadcasted_iota(jnp.int32, (8, BS), 1)

    def gram_copy(d):
        return pltpu.make_async_remote_copy(
            src_ref=gs, dst_ref=gr.at[d], send_sem=s5.at[d], recv_sem=r5.at[d],
            device_id={"wide": up_peer(d)}, device_id_type=MESH,
        )

    def gram_sum(value):
        gs[:, : 2 * R] = value
        gr[0, :, : 2 * R] = value
        for d in range(1, W):
            gram_copy(d).start()
        for d in range(1, W):
            gram_copy(d).wait_recv()
        summed = jnp.zeros((2 * R, 2 * R), jnp.float32)
        for s in range(W):
            summed += gr[lax.rem(me - s + W, W)][:, : 2 * R]
        for d in range(1, W):
            gram_copy(d).wait_send()
        return summed / total

    gs[...] = jnp.zeros_like(gs)
    xs[:R, :] = q_ref[...]
    xs[R:, :] = jnp.zeros((R, B * BS), jnp.float32)
    prev[...] = jnp.zeros_like(prev)
    up[...] = jnp.zeros_like(up)
    start = gram_sum(dot_nt(xs[...], xs[...], HIGH))
    _, _, inverse0 = factor_of(start[:R, :R], R)
    xs[:R, :] = dot32(inverse0, q_ref[...])

    def step(k, carry):
        for b in range(B):
            value = xs[:R, b * BS : (b + 1) * BS]
            blocks[b] = value
            whole, unit_of = coded(value)
            coded_blocks[b] = whole
            scales[b] = jnp.broadcast_to(unit_of, (R, BS))
        for d in range(W):
            spread = jnp.zeros((R, BS), jnp.float32)
            for c in range(C):
                value = coded_blocks[local[d * C + c]]
                (rb if d == 0 else sb)[pl.ds((d * C + c) * R, R), :] = value
                spread = jnp.where(lane == c, scales[local[d * C + c]], spread)
            (rs1 if d == 0 else ss)[pl.ds(d * R, R), :] = spread
            if d:
                request(d).start()
                request_scale(d).start()

        def group(d, carry):
            @pl.when(d > 0)
            def _():
                request(d).wait_recv()
                request_scale(d).wait_recv()

            scale_rows = pl.ds(pl.multiple_of(d * R, R), R)
            scale = rs1[scale_rows, :]
            spread = jnp.zeros((R, BS), jnp.float32)
            for c in range(C):
                p = d * C + c
                rows = pl.ds(pl.multiple_of(p * R, R), R)
                tile = tiles[p]
                high, low = split(number(rb[rows, :]))
                left = jnp.concatenate(
                    [
                        jnp.concatenate([high, high], axis=1),
                        jnp.concatenate([low, jnp.zeros_like(low)], axis=1),
                    ],
                    axis=0,
                )
                both = dot_nt(left, tile)
                tf[rows, :] = (both[:R] + both[R:]) * scale[:, c : c + 1]
                high, low = split(blocks[first[p]])
                both = jnp.dot(
                    jnp.concatenate([high, low], axis=0), tile, preferred_element_type=jnp.float32
                )
                whole, unit_of = coded(both[:R, :BS] + both[R:, :BS] + both[:R, BS:])
                sb2[rows, :] = whole
                spread = jnp.where(lane == c, unit_of, spread)
            ss2[scale_rows, :] = spread

            @pl.when(d > 0)
            def _():
                answer(d).start()
                answer_scale(d).start()

            return carry

        lax.fori_loop(0, W, group, 0)
        for d in range(W):
            if d:
                answer(d).wait_recv()
                answer_scale(d).wait_recv()
            scale = (rs2 if d else ss2)[pl.ds(d * R, R), :]
            for c in range(C):
                rows = pl.ds((d * C + c) * R, R)
                rb2[rows, :] = number((rq if d else sb2)[rows, :]) * scale[:, c : c + 1]

        one_hot = owners[...]
        for n in range(1, N + 1):
            part = lax.rem(nar + n, N)
            spread = jnp.zeros((8, BS), jnp.float32)
            for q in range(RN):
                r = part * RN + q
                x = jnp.concatenate(
                    [tf[pl.ds(r, W * C, stride=R), :], rb2[pl.ds(r, W * C, stride=R), :]], axis=0
                )
                high, low = split(x)
                value = jnp.dot(
                    one_hot,
                    jnp.concatenate([high, low], axis=0),
                    preferred_element_type=jnp.float32,
                )
                if n == N:
                    acc[pl.ds(q * B, B), :] = value
                else:
                    whole, unit_of = coded(value, (0, 1))
                    pb[pl.ds(pl.multiple_of(part * PR + q * B, B), B), :] = whole
                    spread = jnp.where(lane8 == q, unit_of, spread)
            if n < N:
                psc[n] = spread
                scatter(n).start()
                scatter_scale(n).start()
        for d in range(1, N):
            scatter(d).wait_recv()
            scatter_scale(d).wait_recv()
        spread = jnp.zeros((8, BS), jnp.float32)
        for q in range(RN):
            rows = pl.ds(q * B, B)
            value = acc[rows, :]
            for d in range(1, N):
                value += number(rs[d, rows, :]) * rsc[d][:1, q : q + 1]
            whole, unit_of = coded(value, (0, 1))
            out16[rows, :] = whole
            all16[pl.ds(pl.multiple_of(nar * PR + q * B, B), B), :] = whole
            spread = jnp.where(lane8 == q, unit_of, spread)
        osc[...] = spread
        asc[nar] = spread
        for d in range(1, N):
            gather(d).start()
            gather_scale(d, nar).start()
        for d in range(1, N):
            gathered(d).wait_recv()
            gather_scale(d, lax.rem(nar - d + N, N)).wait_recv()
        for r in range(R):
            rows = pl.ds(r * B, B)
            unit_of = asc[r // RN][:1, r % RN : r % RN + 1]
            ag[rows, :] = number(all16[rows, :]) * unit_of

        for b in range(B):
            xs[R:, b * BS : (b + 1) * BS] = ag[pl.ds(b, R, stride=B), :]
        xs[R:, :] = xs[R:, :] - dot32(up[...], prev[...])
        summed = gram_sum(dot_nt(xs[...], xs[...], HIGH))
        basis_gram = summed[:R, :R]
        along = summed[:R, R:]
        along_t = summed[R:, :R]
        raw = summed[R:, R:]
        gram = raw - 2.0 * dot32(along_t, along) + dot32(along_t, dot32(basis_gram, along))
        lower, upper, inverse = factor_of(gram, R)
        coef[k, 0] = along
        coef[k, 1] = lower
        prev[...] = xs[:R, :]
        up[...] = upper
        mix = jnp.concatenate([-dot32(inverse, along_t), inverse], axis=1)
        xs[:R, :] = dot32(mix, xs[...])

        for d in range(1, W):
            request(d).wait_send()
            answer(d).wait_send()
            request_scale(d).wait_send()
            answer_scale(d).wait_send()
        for d in range(1, N):
            scatter(d).wait_send()
            gather(d).wait_send()
            scatter_scale(d).wait_send()
            gather_scale(d, nar).wait_send()
        return carry

    lax.fori_loop(0, STEPS, step, 0)
    out[...] = xs[:R, :]


def quarter_scale(code):
    return jnp.exp(code.astype(jnp.float32) * (1.0 / LOG_STEPS))


def packed(values):
    top = jnp.abs(values[0])
    for value in values[1:]:
        top = jnp.maximum(top, jnp.abs(value))
    top = jnp.maximum(jnp.max(top, axis=1, keepdims=True), 1e-30)
    whole = jnp.ceil(jnp.log(top) * LOG_STEPS).astype(jnp.int32)
    whole = jnp.broadcast_to(whole, values[0].shape)
    factor = LEVELS / quarter_scale(whole)
    out = [
        jnp.clip(jnp.round(value * factor), -LEVELS, LEVELS).astype(jnp.int32).astype(jnp.int16)
        for value in values
    ]
    return out + [whole.astype(jnp.int16)]


SLOTS = 5
Z_ROWS = 48
PARTS = 4


def fused_kernel(dims, names, points, q_ref, pairs_ref, out, coef, *refs):
    W, N, C, R, B, F, total = dims
    s_ = dict(zip(names, refs))
    (unit, uq0, uq1, uq2, uq3, uq4, kt, tf1, tf2, vo, vr, rep, perm, shift, yt, zt, oht1, oht2, oh1, oh2, lv, ls, idx_i, idx_j, idx_v, n2, w2, o1n, o1w, i1n, i1w,
     y1, y2, gs, gn, gt, gw, qc, pv, wp, zp, at, inv, up) = (s_[n] for n in DATA)
    sem = s_
    uq = (uq0, uq1, uq2, uq3, uq4)
    QR = BS // N
    JQ = B // N
    HALF = W * C
    me = lax.axis_index("wide")
    nar = lax.axis_index("narrow")
    z, x = lax.div(me, 2), lax.rem(me, 2)
    h = lax.div(z, 2)
    e = lax.rem(z, 2)
    cd = (1 - h) * (3 - z) + h * (z - 2)
    cs = (1 - h) * (z + 2) + h * (3 - z)
    ax = 1 - x
    side = z + 1 - 2 * e
    XN = 2 * z + ax
    SRC = [XN, 2 * cs + x, 2 * cs + ax, 2 * side + (1 - e) * ax + e * x]
    DST = [XN, 2 * cd + x, 2 * cd + ax, 2 * side + (1 - e) * x + e * ax]
    GROUP = [me] + SRC
    lane = lax.broadcasted_iota(jnp.int32, (R, BS), 1)
    lane8 = lax.broadcasted_iota(jnp.int32, (8, BS), 1)
    sub8 = lax.broadcasted_iota(jnp.int32, (8, BS), 0)

    def slot_is(s, lanes=None):
        lanes = lane if lanes is None else lanes
        return (lanes >= s * QR) & (lanes < s * QR + QR)

    def filled(value):
        value = value + pltpu.roll(value, QR, 1)
        return value + pltpu.roll(value, 2 * QR, 1)

    def remote(src, dst, name, at_, where):
        return pltpu.make_async_remote_copy(
            src_ref=src, dst_ref=dst, send_sem=sem["s_" + name].at[at_], recv_sem=sem["r_" + name].at[at_],
            device_id=where, device_id_type=MESH,
        )

    def wide(d):
        return {"wide": d}

    def nearby(d):
        return {"narrow": lax.rem(nar + d, N)}

    def behind(d):
        return lax.rem(nar - d + N, N)

    PART = B // PARTS

    def part(s, t):
        return uq[s].at[pl.ds(t * PART, PART)]

    def hop_x(t):
        return remote(part(0, t), part(1, t), "px", t, wide(XN))

    def hop_c(t):
        return remote(part(0, t), part(2, t), "pc", t, wide(DST[1]))

    def hop_f(t):
        return remote(part(2, t), part(3, t), "pf", t, wide(XN))

    def hop_a(t, s=0):
        return remote(part(s, t), part(4, t), "pa", t, wide(2 * side + x))

    def list_near(d):
        return remote(pairs_ref, lv.at[0, nar], "ln", d, nearby(d))

    def list_wide(d):
        return remote(lv.at[0], lv.at[d], "lw", d, wide(DST[d]))

    def vec_near(k, d):
        return remote(n2.at[k, nar], n2.at[k, nar], "vn", (k, d), nearby(d))

    def vec_near_in(k, d):
        place = n2.at[k, behind(d)]
        return remote(place, place, "vn", (k, d), nearby(d))

    def vec_wide(k, d):
        return remote(n2.at[k, nar], w2.at[k, d], "vw", (k, d), wide(DST[d]))

    def sum_near(k, d):
        return remote(o1n.at[k, d], i1n.at[k, d], "sn", (k, d), nearby(d))

    def sum_wide(k, d):
        return remote(o1w.at[k, d], i1w.at[k, d], "sw", (k, d), wide(SRC[d]))

    def gram_near(k, d):
        return remote(gs.at[k], gn.at[k, nar], "gn", (k, d), nearby(d))

    def gram_near_in(k, d):
        place = gn.at[k, behind(d)]
        return remote(place, place, "gn", (k, d), nearby(d))

    def gram_wide(k, d):
        return remote(gt.at[k], gw.at[k, me], "gw", (k, d), wide(lax.rem(me + d, W)))

    def gram_wide_in(k, d):
        place = gw.at[k, lax.rem(me - d + W, W)]
        return remote(place, place, "gw", (k, d), wide(lax.rem(me + d, W)))

    barrier = pltpu.get_barrier_semaphore()
    for d in range(1, W):
        pl.semaphore_signal(barrier, inc=1, device_id=wide(lax.rem(me + d, W)), device_id_type=MESH)
    for d in range(1, N):
        pl.semaphore_signal(barrier, inc=1, device_id=nearby(d), device_id_type=MESH)

    def normalise(b, carry):
        unit[b] = unit_rows(points[pl.ds(pl.multiple_of(b * BS, BS), BS), :])
        return carry

    def quarter(b, carry):
        uq0[b] = unit_rows(points[pl.ds(pl.multiple_of(b * BS + nar * QR, QR), QR), :])
        return carry

    lax.fori_loop(0, B, quarter, 0, unroll=4)

    def square(x_):
        four = jnp.concatenate([x_] * (BS // (2 * R)), axis=0)
        full = dot_nt(x_, four, HIGH)
        small = jnp.zeros((8, BS), jnp.float32)
        for a in range(2 * R // 8):
            small = jnp.where(slot_is(a, lane8), full[8 * a : 8 * a + 8], small)
        return small

    def gram_value(k):
        total_ = gw[k, 0]
        for d in range(1, W):
            total_ = total_ + gw[k, d]
        rows = [total_] + [pltpu.roll(total_, BS - a * 2 * R, 1) for a in range(1, 2 * R // 8)]
        return jnp.concatenate(rows, axis=0)[:, : 2 * R] / total

    def gram_send(k):
        gw[k, me] = gt[k]
        for d in range(1, W):
            gram_wide(k, d).start()

    def gram_collect(k):
        for d in range(1, N):
            gram_near_in(k, d).wait_recv()
        value = gn[k, 0]
        for d in range(1, N):
            value = value + gn[k, d]
        gt[k] = value
        gram_send(k)

    def gram_start(k):
        value = square(jnp.concatenate([qc[...], wp[...]], axis=0))
        gs[k] = value
        gn[k, nar] = value
        for d in range(1, N):
            gram_near(k, d).start()

    def gram_finish(k):
        for d in range(1, W):
            gram_wide_in(k, d).wait_recv()
        summed = gram_value(k)
        along = summed[:R, R:]
        along_t = summed[R:, :R]
        gram = summed[R:, R:] - 2.0 * dot32(along_t, along) + dot32(along_t, dot32(summed[:R, :R], along))
        lower, upper, inverse = factor_of(gram, R)
        coef[k - 1, 0] = along
        coef[k - 1, 1] = lower
        at[...] = along_t
        inv[...] = inverse
        up[...] = upper
        pv[...] = qc[...]
        qc[...] = dot32(inverse, wp[...] - dot32(along_t, qc[...]))

    lv[0, nar] = pairs_ref[...]
    q_all = q_ref[...]
    gt[0] = square(jnp.concatenate([q_all, q_all], axis=0))
    pl.semaphore_wait(barrier, W - 1 + N - 1)

    for d in range(1, N):
        list_near(d).start()
    gram_send(0)
    hop_c(0).start()
    hop_x(0).start()
    for d in range(1, N):
        place = lv.at[0, behind(d)]
        remote(place, place, "ln", d, nearby(d)).wait_recv()
    for d in range(1, 4):
        list_wide(d).start()
    for t in range(1, PARTS):
        hop_c(t).start()
        hop_x(t).start()

    @pl.when(e == 0)
    def _():
        for t in range(PARTS):
            hop_a(t).start()

    def relay_x(t):
        hop_x(t).wait_recv()

        @pl.when(e == 1)
        def _():
            hop_a(t, 1).start()

    def relay_c(t):
        hop_c(t).wait_recv()
        hop_f(t).start()

    lax.fori_loop(0, B, normalise, 0, unroll=2)

    def places(rows, columns, of):
        row = lax.broadcasted_iota(jnp.int32, (rows, columns), 0)
        column = lax.broadcasted_iota(jnp.int32, (rows, columns), 1)
        return (row == of(column)).astype(jnp.float32).astype(jnp.bfloat16)

    rep[...] = places(BS, N * BS, lambda l: (l // BS) * QR + (l & (QR - 1)))
    perm[...] = places(
        N * BS, N * BS, lambda l: ((l // QR) & (N - 1)) * BS + (l // BS) * QR + (l & (QR - 1))
    )
    for a in range(N):
        shift[a * BS : (a + 1) * BS, :] = places(
            BS, BS, lambda l: ((l // QR + N - a) & (N - 1)) * QR + (l & (QR - 1))
        )

    relay_x(0)
    for jq in range(JQ):
        value = jnp.zeros((R, BS), jnp.float32)
        for s in range(N):
            b = N * jq + s
            one = filled(jnp.where(slot_is(nar), q_ref[:, b * BS : (b + 1) * BS], 0.0))
            value = jnp.where(slot_is(s), one, value)
        wp[:, jq * BS : (jq + 1) * BS] = value

    for d in range(1, W):
        gram_wide_in(0, d).wait_recv()
    _, _, inverse0 = factor_of(gram_value(0)[:R, :R], R)
    qc[...] = dot32(inverse0, wp[...])
    for ref in (pv, zp, at, up):
        ref[...] = jnp.zeros_like(ref)
    inv[...] = (
        lax.broadcasted_iota(jnp.int32, (R, R), 0) == lax.broadcasted_iota(jnp.int32, (R, R), 1)
    ).astype(jnp.float32)

    def lanes_of(ref):
        return [ref[:, jq * BS : (jq + 1) * BS] for jq in range(JQ)]

    def vec_send(k, ref):
        for jq, value in enumerate(packed(lanes_of(ref))):
            n2[k, nar, jq * R : (jq + 1) * R, :] = value
        for d in range(1, N):
            vec_near(k, d).start()
        for d in range(4):
            vec_wide(k, d).start()

    vec_send(0, qc)
    relay_x(1)
    relay_c(0)
    for d in range(1, 4):
        remote(lv.at[d], lv.at[d], "lw", d, wide(DST[d])).wait_recv()
    local = pltpu.make_async_copy(lv, ls, sem["m_ls"])
    local.start()
    local.wait()

    kinds = []
    for s in range(SLOTS):
        kinds.append((s, 0))
        if s > 1:
            kinds.append((s, 1))

    for at_kind, (s, kind) in enumerate(kinds):
        other = GROUP[s]

        def indices(mq, carry):
            ch = at_kind * N + mq
            vi = jnp.zeros((8, BS), jnp.int32)
            vj = jnp.zeros((8, BS), jnp.int32)
            for c in range(C):
                if kind == 0:
                    i = lax.rem(ls[0, mq, 0, other * C + c], B)
                    j = lax.rem(ls[0, mq, 0, HALF + other * C + c], B)
                else:
                    j = lax.rem(ls[s - 1, mq, 0, me * C + c], B)
                    i = lax.rem(ls[s - 1, mq, 0, HALF + me * C + c], B)
                idx_i[ch * C + c] = i
                idx_j[ch * C + c] = j
                idx_v[ch * C + c] = s * B + j
                vi = jnp.where(sub8 == c, i, vi)
                vj = jnp.where(sub8 == c, j, vj)
            rows = pl.ds(pl.multiple_of(ch * C, C), C)
            row = (vi & (N - 1)) * JQ + vi // N
            oht1[rows, :] = (row == lane8).astype(jnp.float32)
            row = ((vj + N - (sub8 & (N - 1))) & (N - 1)) * Z_ROWS + s * JQ + vj // N
            oht2[rows, :BS] = (row == lane8).astype(jnp.float32)
            oht2[rows, BS:] = (row == lane8 + BS).astype(jnp.float32)
            return carry

        lax.fori_loop(0, N, indices, 0)

    relay_x(2)
    relay_c(1)
    turned = jnp.transpose(oht1[...])[: oh1.shape[0]].astype(jnp.bfloat16)
    oh1[...] = jnp.concatenate([turned, turned], axis=1)
    turned = jnp.transpose(oht2[...])[: oh2.shape[0]].astype(jnp.bfloat16)
    oh2[...] = jnp.concatenate([turned, turned], axis=1)

    def tiles_of(want):
        for at_kind, (s, kind) in enumerate(kinds):
            if s != want:
                continue

            def make(mq, carry):
                ch = at_kind * N + mq
                for c in range(C):
                    p = ch * C + c
                    sim = dot_nt(uq[s][idx_j[p]], unit[idx_i[p]])
                    high, low = split(jnp.exp(KERNEL_FACTOR * (sim - 1.0)))
                    rows = pl.ds(pl.multiple_of(p * QR, QR), QR)
                    kt[rows, :BS] = high
                    kt[rows, BS:] = low
                return carry

            lax.fori_loop(0, N, make, 0, unroll=2)

    tiles_of(0)
    relay_x(3)
    relay_c(2)
    tiles_of(1)
    relay_c(3)
    tiles_of(2)
    for t in range(PARTS):
        hop_a(t).wait_recv()
    tiles_of(4)
    for t in range(PARTS):
        hop_f(t).wait_recv()
    tiles_of(3)

    chunks = len(kinds) * N

    def unpacked(ref, k, d):
        scale = quarter_scale(ref[k, d, JQ * R : (JQ + 1) * R, :].astype(jnp.int32)) * (1.0 / LEVELS)
        return [number(ref[k, d, jq * R : (jq + 1) * R, :]) * scale for jq in range(JQ)]

    def both(value):
        return jnp.concatenate(split(value), axis=0)

    def scatter(tf, one_hot, keep):
        for r in range(0, R, 2):
            columns = []
            for q in range(2):
                high, low = split(tf[pl.ds(r + q, chunks * C, stride=R), :])
                columns.append(jnp.concatenate([high, low], axis=0))
            value = jnp.dot(
                one_hot[...], jnp.concatenate(columns, axis=1), preferred_element_type=jnp.float32
            )
            keep(r, value[:, :BS])
            keep(r + 1, value[:, BS:])

    def moved(value, matrix):
        rows = value.shape[0]
        value = jnp.dot(both(value), matrix[...], preferred_element_type=jnp.float32)
        return value[:rows] + value[rows:]

    def step(k, carry):
        for d in range(1, N):
            vec_near_in(k, d).wait_recv()
        quarters = [unpacked(n2, k, q) for q in range(N)]
        pieces = [
            jnp.concatenate([both(quarters[q][jq]) for q in range(N)], axis=1) for jq in range(JQ)
        ]
        value = jnp.dot(jnp.concatenate(pieces, axis=0), perm[...], preferred_element_type=jnp.float32)
        value = value.astype(jnp.bfloat16)
        for jq in range(JQ):
            for s in range(N):
                vo[jq * N + s] = value[2 * R * jq : 2 * R * (jq + 1), s * BS : (s + 1) * BS]
        mine = unpacked(n2, k, nar)

        def keep_remote(s, values):
            value = jnp.dot(
                jnp.concatenate([both(v) for v in values], axis=0), rep[...],
                preferred_element_type=jnp.float32,
            ).astype(jnp.bfloat16)
            for jq in range(JQ):
                for b in range(N):
                    vr[s * B + jq * N + b] = value[2 * R * jq : 2 * R * (jq + 1), b * BS : (b + 1) * BS]

        keep_remote(0, mine)

        @pl.when(k > 0)
        def _():
            gram_collect(k)

        def second(ch, carry):
            left = jnp.concatenate([vo[idx_i[ch * C + c]] for c in range(C)], axis=0)
            tile = kt[pl.ds(pl.multiple_of(ch * C * QR, C * QR), C * QR), :]
            full = dot_nt(jnp.concatenate([left, left], axis=1), tile)
            for c in range(C):
                columns = slice((c // N) * BS, (c // N + 1) * BS)
                value = full[2 * R * c : 2 * R * c + R, columns] + full[2 * R * c + R : 2 * R * (c + 1), columns]
                value = jnp.where(slot_is(c % N), value, 0.0)
                tf2[pl.ds(pl.multiple_of((ch * C + c) * R, R), R), :] = value
            return carry

        lax.fori_loop(0, chunks, second, 0, unroll=8)

        def keep2(r, value):
            for a in range(N):
                zt[r * SLOTS * JQ : (r + 1) * SLOTS * JQ, a * BS : (a + 1) * BS] = (
                    value[a * Z_ROWS : a * Z_ROWS + SLOTS * JQ]
                )

        scatter(tf2, oh2, keep2)
        batch = R // 4
        for first_r in range(0, R, batch):
            value = moved(zt[first_r * SLOTS * JQ : (first_r + batch) * SLOTS * JQ, :], shift)
            for r in range(batch):
                for s in range(SLOTS):
                    place = (r * SLOTS + s) * JQ
                    y2[s, pl.ds(first_r + r, JQ, stride=R), :] = value[place : place + JQ]
        for d in range(4):
            for jq, value in enumerate(packed([y2[d + 1, jq * R : (jq + 1) * R, :] for jq in range(JQ)])):
                o1w[k, d, jq * R : (jq + 1) * R, :] = value
            sum_wide(k, d).start()

        for d in range(4):
            remote(w2.at[k, d], w2.at[k, d], "vw", (k, d), wide(DST[d])).wait_recv()
            keep_remote(d + 1, unpacked(w2, k, d))

        def first(ch, carry):
            left = []
            for c in range(C):
                value = vr[idx_v[ch * C + c]]
                value = jnp.where(slot_is(c % N, lane2), value, jnp.zeros_like(value))
                pieces = [jnp.zeros_like(value)] * (C // N)
                pieces[c // N] = value
                left.append(jnp.concatenate(pieces, axis=1))
            tile = kt[pl.ds(pl.multiple_of(ch * C * QR, C * QR), C * QR), :]
            full = jnp.dot(jnp.concatenate(left, axis=0), tile, preferred_element_type=jnp.float32)
            for c in range(C):
                high = full[2 * R * c : 2 * R * c + R]
                low = full[2 * R * c + R : 2 * R * (c + 1)]
                tf1[pl.ds(pl.multiple_of((ch * C + c) * R, R), R), :] = (
                    high[:, :BS] + high[:, BS:] + low[:, :BS]
                )
            return carry

        lax.fori_loop(0, chunks, first, 0, unroll=8)

        def keep1(r, value):
            for s in range(N):
                yt[r * JQ : (r + 1) * JQ, s * BS : (s + 1) * BS] = value[s * JQ : (s + 1) * JQ]

        scatter(tf1, oh1, keep1)
        value = moved(yt[...], perm)
        for r in range(R):
            for q in range(N):
                y1[q, pl.ds(r, JQ, stride=R), :] = value[r * JQ : (r + 1) * JQ, q * BS : (q + 1) * BS]

        for d in range(1, N):
            to = lax.rem(nar + d, N)
            for jq, value in enumerate(packed([y1[to, jq * R : (jq + 1) * R, :] for jq in range(JQ)])):
                o1n[k, d, jq * R : (jq + 1) * R, :] = value
            sum_near(k, d).start()

        @pl.when(k > 0)
        def _():
            gram_finish(k)

        image = [y1[nar, jq * R : (jq + 1) * R, :] + y2[0, jq * R : (jq + 1) * R, :] for jq in range(JQ)]
        for d in range(4):
            sum_wide(k, d).wait_recv()
            image = [a + b for a, b in zip(image, unpacked(i1w, k, d))]
        for d in range(1, N):
            sum_near(k, d).wait_recv()
            image = [a + b for a, b in zip(image, unpacked(i1n, k, d))]
        image = jnp.concatenate(image, axis=1)
        image = dot32(inv[...], image - dot32(at[...], zp[...]))
        zp[...] = image
        wp[...] = image - dot32(up[...], pv[...])

        @pl.when(k < STEPS - 1)
        def _():
            vec_send(k + 1, wp)

        gram_start(k + 1)
        return carry

    lane2 = lax.broadcasted_iota(jnp.int32, (2 * R, BS), 1)
    lax.fori_loop(0, STEPS, step, 0)
    gram_collect(STEPS)
    gram_finish(STEPS)
    for jq, value in enumerate(packed(lanes_of(qc))):
        n2[STEPS, nar, jq * R : (jq + 1) * R, :] = value
    for d in range(1, N):
        vec_near(STEPS, d).start()
    for d in range(1, N):
        vec_near_in(STEPS, d).wait_recv()
    pieces = [jnp.concatenate(unpacked(n2, STEPS, q), axis=0) for q in range(N)]
    value = moved(jnp.concatenate(pieces, axis=1), perm)
    for jq in range(JQ):
        for s in range(N):
            b = jq * N + s
            out[:, b * BS : (b + 1) * BS] = value[jq * R : (jq + 1) * R, s * BS : (s + 1) * BS]

    for t in range(PARTS):
        hop_x(t).wait_send()
        hop_c(t).wait_send()
        hop_a(t).wait_send()
        hop_f(t).wait_send()
    for d in range(1, N):
        list_near(d).wait_send()
        vec_near(STEPS, d).wait_send()
    for d in range(1, 4):
        list_wide(d).wait_send()
    for d in range(1, W):
        gram_wide(0, d).wait_send()
    for k in range(STEPS):
        for d in range(1, N):
            vec_near(k, d).wait_send()
            sum_near(k, d).wait_send()
            gram_near(k + 1, d).wait_send()
        for d in range(4):
            vec_wide(k, d).wait_send()
            sum_wide(k, d).wait_send()
        for d in range(1, W):
            gram_wide(k + 1, d).wait_send()


DATA = (
    "unit", "uq0", "uq1", "uq2", "uq3", "uq4", "kt", "tf1", "tf2", "vo", "vr", "rep", "perm", "shift", "yt", "zt", "oht1", "oht2",
    "oh1", "oh2", "lv", "ls", "idx_i", "idx_j", "idx_v", "n2", "w2", "o1n", "o1w", "i1n", "i1w", "y1", "y2",
    "gs", "gn", "gt", "gw", "qc", "pv", "wp", "zp", "at", "inv", "up",
)


def fused(points, q_init, pairs, W, N):
    R, cols = q_init.shape
    F = points.shape[1]
    B = cols // BS
    pair_count = pairs.shape[1]
    C = pair_count // W
    QR, JQ = BS // N, B // N
    P_ = (SLOTS + SLOTS - 2) * N * C
    f32, bf16, i16, i32 = jnp.float32, jnp.bfloat16, jnp.int16, jnp.int32
    V = pltpu.VMEM
    message = ((JQ + 1) * R, BS)
    rounds = STEPS + 1
    columns = JQ * BS
    shapes = {
        "unit": V((B, BS, F), bf16), **{f"uq{s}": V((B, QR, F), bf16) for s in range(SLOTS)}, "kt": V((P_ * QR, 2 * BS), bf16),
        "tf1": V((P_ * R, BS), f32), "tf2": V((P_ * R, BS), f32),
        "vo": V((B, 2 * R, BS), bf16), "vr": V((SLOTS * B, 2 * R, BS), bf16),
        "oht1": V((P_, BS), f32), "oht2": V((P_, 2 * BS), f32),
        "rep": V((BS, N * BS), bf16), "perm": V((N * BS, N * BS), bf16), "shift": V((N * BS, BS), bf16),
        "yt": V((R * JQ, N * BS), f32), "zt": V((R * SLOTS * JQ, N * BS), f32),
        "oh1": V((B, 2 * P_), bf16), "oh2": V((N * Z_ROWS, 2 * P_), bf16),
        "lv": V((4, N, 1, 2 * pair_count), i32), "ls": pltpu.SMEM((4, N, 1, 2 * pair_count), i32),
        "idx_i": pltpu.SMEM((P_,), i32), "idx_j": pltpu.SMEM((P_,), i32),
        "idx_v": pltpu.SMEM((P_,), i32),
        "n2": V((rounds, N) + message, i16), "w2": V((STEPS, 4) + message, i16),
        "o1n": V((STEPS, N) + message, i16), "o1w": V((STEPS, 4) + message, i16),
        "i1n": V((STEPS, N) + message, i16), "i1w": V((STEPS, 4) + message, i16),
        "y1": V((N, JQ * R, BS), f32), "y2": V((SLOTS, JQ * R, BS), f32),
        "gs": V((rounds, 8, BS), f32), "gn": V((rounds, N, 8, BS), f32),
        "gt": V((rounds, 8, BS), f32), "gw": V((rounds, W, 8, BS), f32),
        "qc": V((R, columns), f32), "pv": V((R, columns), f32), "wp": V((R, columns), f32),
        "zp": V((R, columns), f32),
        "at": V((R, R), f32), "inv": V((R, R), f32), "up": V((R, R), f32),
    }
    sems = {
        "px": (PARTS,), "pc": (PARTS,), "pf": (PARTS,), "pa": (PARTS,), "ln": (N,), "lw": (4,),
        "vn": (rounds, N), "vw": (STEPS, 4), "sn": (STEPS, N), "sw": (STEPS, 4),
        "gn": (rounds, N), "gw": (rounds, W),
    }
    names = list(DATA)
    scratch = [shapes[n] for n in DATA]
    for name, shape in sems.items():
        for way in "sr":
            names.append(way + "_" + name)
            scratch.append(pltpu.SemaphoreType.DMA(shape))
    names.append("m_ls")
    scratch.append(pltpu.SemaphoreType.DMA)
    vmem = pl.BlockSpec(memory_space=pltpu.VMEM)
    dims = (W, N, C, R, B, F, B * BS * W)
    return pl.pallas_call(
        functools.partial(fused_kernel, dims, tuple(names)),
        out_shape=(
            jax.ShapeDtypeStruct((R, cols), f32),
            jax.ShapeDtypeStruct((STEPS, 2, R, R), f32),
        ),
        in_specs=[vmem, vmem, vmem],
        out_specs=(vmem, vmem),
        scratch_shapes=scratch,
        compiler_params=pltpu.CompilerParams(collective_id=1, has_side_effects=True),
        name="fused",
    )(points, q_init, pairs.reshape(1, 2 * pair_count))


def lanczos(first, local, owners, tiles, q_init, wide_count, narrow_count, total):
    R, cols = q_init.shape
    B = cols // BS
    pair_count = first.shape[0]
    C = pair_count // wide_count
    dims = (wide_count, narrow_count, C, R, B, total)
    vmem = pl.BlockSpec(memory_space=pltpu.VMEM)
    smem = pl.BlockSpec(memory_space=pltpu.SMEM)
    f32 = jnp.float32
    pairs_buf = pltpu.VMEM((pair_count * R, BS), f32)
    coded_buf = pltpu.VMEM((pair_count * R, BS), jnp.int16)
    scale_buf = pltpu.VMEM((wide_count * R, BS), f32)
    part = R // narrow_count * B
    wide_sem = pltpu.SemaphoreType.DMA((wide_count,))
    narrow_sem = pltpu.SemaphoreType.DMA((narrow_count,))
    return pl.pallas_call(
        functools.partial(main_kernel, dims),
        out_shape=(
            jax.ShapeDtypeStruct((R, cols), f32),
            jax.ShapeDtypeStruct((STEPS, 2, R, R), f32),
        ),
        in_specs=[smem, smem, vmem, vmem, vmem],
        out_specs=(vmem, vmem),
        scratch_shapes=[
            coded_buf, coded_buf, coded_buf, coded_buf,
            scale_buf, scale_buf, scale_buf, scale_buf,
            pltpu.VMEM((B, R, BS), jnp.int16),
            pltpu.VMEM((B, R, BS), f32),
            pairs_buf, pairs_buf,
            pltpu.VMEM((R * B, BS), jnp.int16),
            pltpu.VMEM((narrow_count, part, BS), jnp.int16),
            pltpu.VMEM((R * B, BS), f32),
            pltpu.VMEM((part, BS), f32),
            pltpu.VMEM((part, BS), jnp.int16),
            pltpu.VMEM((R * B, BS), jnp.int16),
            pltpu.VMEM((narrow_count, 8, BS), f32),
            pltpu.VMEM((narrow_count, 8, BS), f32),
            pltpu.VMEM((8, BS), f32),
            pltpu.VMEM((narrow_count, 8, BS), f32),
            pltpu.VMEM((2 * R, cols), f32),
            pltpu.VMEM((B, R, BS), f32),
            pltpu.VMEM((R, cols), f32),
            pltpu.VMEM((R, R), f32),
            pltpu.VMEM((2 * R, BS), f32),
            pltpu.VMEM((wide_count, 2 * R, BS), f32),
            wide_sem, wide_sem, wide_sem, wide_sem,
            narrow_sem, narrow_sem, narrow_sem, narrow_sem,
            wide_sem, wide_sem, wide_sem, wide_sem, wide_sem, wide_sem,
            narrow_sem, narrow_sem, narrow_sem, narrow_sem,
        ],
        compiler_params=pltpu.CompilerParams(collective_id=0, has_side_effects=True),
        name="lanczos",
    )(first, local, owners, tiles, q_init)


def per_device(points, q_init, pairs):
    wide_count = lax.axis_size("wide")
    narrow_count = lax.axis_size("narrow")
    me = lax.axis_index("wide")
    own_blocks = points.shape[0] // BS
    width = points.shape[1]
    pair_count = pairs.shape[1]
    capacity = pair_count // wide_count
    if wide_count == 8 and narrow_count == 4 and own_blocks == 8 * narrow_count and capacity == 8:
        return fused(points, q_init, pairs, wide_count, narrow_count)
    total = own_blocks * BS * wide_count
    unit = unit_rows(points).reshape(own_blocks, BS, width)
    turn = jnp.arange(wide_count, dtype=jnp.int32)
    first_rows = (pairs[0] - me * own_blocks).reshape(wide_count, capacity)
    first = first_rows[(me - turn) % wide_count].reshape(pair_count)
    second = (pairs[1].reshape(wide_count, capacity) - turn[:, None] * own_blocks)
    every = lax.all_to_all(
        jnp.broadcast_to(second.reshape(1, pair_count), (wide_count, pair_count)),
        "wide", split_axis=0, concat_axis=0, tiled=True,
    ).reshape(wide_count, wide_count, capacity)
    local_ids = lax.dynamic_index_in_dim(every, me, axis=1, keepdims=False)
    local = local_ids[(me + turn) % wide_count].reshape(pair_count)
    targets = jnp.concatenate([first, local, first, local])
    owners = (jnp.arange(own_blocks, dtype=jnp.int32)[:, None] == targets[None, :]).astype(
        jnp.bfloat16
    )
    blocks = lax.all_to_all(
        unit[local_ids.reshape(pair_count)], "wide", split_axis=0, concat_axis=0, tiled=True
    ).reshape(wide_count, capacity, BS, width)
    tiles = make_tiles(jnp.reshape(me, (1,)).astype(jnp.int32), first, unit, blocks)
    return lanczos(first, local, owners, tiles, q_init, wide_count, narrow_count, total)


def solution(mesh):
    placed = (P("wide", None), P(None, "wide"), P(None, ("wide", "narrow")))
    return jax.shard_map(
        per_device, mesh=mesh, in_specs=placed, out_specs=(P(None, "wide"), P()), check_vma=False
    )
```

```python
import functools

import jax
import jax.numpy as jnp
from jax import lax
from jax.experimental import pallas as pl
from jax.experimental.pallas import tpu as pltpu
from jax.sharding import PartitionSpec as P

BS = 128
STEPS = 3
LEVELS = 32767.0
KERNEL_FACTOR = 3.0
EPSILON = 1e-06
LOG_STEPS = 256.0
HIGH = lax.Precision.HIGHEST
MESH = pl.DeviceIdType.MESH


def unit_rows(points):
    wide32 = points.astype(jnp.float32)
    scaled = wide32 * lax.rsqrt(jnp.sum(wide32 * wide32, axis=-1, keepdims=True) + EPSILON)
    return scaled.astype(jnp.bfloat16)


def split(x):
    high = x.astype(jnp.bfloat16)
    return high, (x - high.astype(jnp.float32)).astype(jnp.bfloat16)


def coded(x, axes=1):
    top = jnp.maximum(jnp.max(jnp.abs(x), axis=axes, keepdims=True), 1e-30)
    scaled = jnp.clip(jnp.round(x * (LEVELS / top)), -LEVELS, LEVELS)
    return scaled.astype(jnp.int32).astype(jnp.int16), top * (1.0 / LEVELS)


def number(x):
    return x.astype(jnp.int32).astype(jnp.float32)


def dot32(a, b):
    return jnp.dot(a, b, precision=HIGH, preferred_element_type=jnp.float32)


def dot_nt(a, b, precision=None):
    return lax.dot_general(
        a, b, (((1,), (1,)), ((), ())), precision=precision, preferred_element_type=jnp.float32
    )


def tiles_kernel(capacity, me_ref, first_ref, unit_ref, second_ref, out_ref):
    d = pl.program_id(0)
    for c in range(capacity):
        s = dot_nt(unit_ref[first_ref[d * capacity + c]], second_ref[0, c])
        high, low = split(jnp.exp(KERNEL_FACTOR * (s - 1.0)))
        out_ref[c, :, :BS] = high
        out_ref[c, :, BS:] = low


def make_tiles(me, first, unit, second):
    wide_count, capacity, _, width = second.shape
    own_blocks = unit.shape[0]
    spec = pltpu.PrefetchScalarGridSpec(
        num_scalar_prefetch=2,
        grid=(wide_count,),
        in_specs=[
            pl.BlockSpec((own_blocks, BS, width), lambda d, m, f: (0, 0, 0)),
            pl.BlockSpec(
                (1, capacity, BS, width),
                lambda d, m, f: (lax.rem(m[0] - d + wide_count, wide_count), 0, 0, 0),
            ),
        ],
        out_specs=pl.BlockSpec((capacity, BS, 2 * BS), lambda d, m, f: (d, 0, 0)),
    )
    return pl.pallas_call(
        functools.partial(tiles_kernel, capacity),
        grid_spec=spec,
        out_shape=jax.ShapeDtypeStruct((wide_count * capacity, BS, 2 * BS), jnp.bfloat16),
        name="tiles",
    )(me, first, unit, second)


def factor_of(gram, r):
    i = lax.broadcasted_iota(jnp.int32, (r, r), 0)
    j = lax.broadcasted_iota(jnp.int32, (r, r), 1)
    both_i = lax.broadcasted_iota(jnp.int32, (r, 2 * r), 0)
    m = jnp.concatenate([gram, (i == j).astype(jnp.float32)], axis=1)
    lower = jnp.zeros((r, r), jnp.float32)
    for k in range(r):
        inv = 1.0 / jnp.sqrt(m[k : k + 1, k : k + 1])
        row = m[k : k + 1, :] * inv
        col = m[:, k : k + 1] * inv
        lower = jnp.where((j == k) & (i >= k), col, lower)
        m = jnp.where(both_i == k, row, jnp.where(both_i > k, m - col * row, m))
    upper = jnp.where(j >= i, m[:, :r], 0.0)
    inverse = jnp.where(j <= i, m[:, r:], 0.0)
    return lower, upper, inverse


def main_kernel(
    dims, first, local, owners, tiles, q_ref, out, coef,
    sb, rb, sb2, rq, ss, rs1, ss2, rs2, coded_blocks, scales, rb2, tf, pb, rs, ag, acc, out16, all16, psc, rsc, osc, asc, xs, blocks, prev, up, gs, gr,
    s1, r1, s2, r2, s3, r3, s4, r4, s5, r5, s6, r6, s7, r7, s8, r8, s9, r9,
):
    W, N, C, R, B, total = dims
    CR = C * R
    RN = R // N
    PR = RN * B
    me = lax.axis_index("wide")
    nar = lax.axis_index("narrow")

    def up_peer(d):
        return lax.rem(me + d, W)

    def down_peer(d):
        return lax.rem(me - d + W, W)

    barrier = pltpu.get_barrier_semaphore()
    for d in range(1, W):
        pl.semaphore_signal(barrier, inc=1, device_id={"wide": up_peer(d)}, device_id_type=MESH)
    for d in range(1, N):
        pl.semaphore_signal(
            barrier, inc=1, device_id={"narrow": lax.rem(nar + d, N)}, device_id_type=MESH
        )
    pl.semaphore_wait(barrier, W - 1 + N - 1)

    def request(d):
        rows = pl.ds(d * CR, CR)
        return pltpu.make_async_remote_copy(
            src_ref=sb.at[rows], dst_ref=rb.at[rows], send_sem=s1.at[d], recv_sem=r1.at[d],
            device_id={"wide": up_peer(d)}, device_id_type=MESH,
        )

    def answer(d):
        rows = pl.ds(d * CR, CR)
        return pltpu.make_async_remote_copy(
            src_ref=sb2.at[rows], dst_ref=rq.at[rows], send_sem=s2.at[d], recv_sem=r2.at[d],
            device_id={"wide": down_peer(d)}, device_id_type=MESH,
        )

    def request_scale(d):
        rows = pl.ds(d * R, R)
        return pltpu.make_async_remote_copy(
            src_ref=ss.at[rows], dst_ref=rs1.at[rows], send_sem=s6.at[d], recv_sem=r6.at[d],
            device_id={"wide": up_peer(d)}, device_id_type=MESH,
        )

    def answer_scale(d):
        rows = pl.ds(d * R, R)
        return pltpu.make_async_remote_copy(
            src_ref=ss2.at[rows], dst_ref=rs2.at[rows], send_sem=s7.at[d], recv_sem=r7.at[d],
            device_id={"wide": down_peer(d)}, device_id_type=MESH,
        )

    lane = lax.broadcasted_iota(jnp.int32, (R, BS), 1)

    def scatter(d):
        return pltpu.make_async_remote_copy(
            src_ref=pb.at[pl.ds(lax.rem(nar + d, N) * PR, PR)], dst_ref=rs.at[d],
            send_sem=s3.at[d], recv_sem=r3.at[d],
            device_id={"narrow": lax.rem(nar + d, N)}, device_id_type=MESH,
        )

    def gather(d):
        mine = pl.ds(nar * PR, PR)
        return pltpu.make_async_remote_copy(
            src_ref=out16, dst_ref=all16.at[mine], send_sem=s4.at[d], recv_sem=r4.at[d],
            device_id={"narrow": lax.rem(nar + d, N)}, device_id_type=MESH,
        )

    def gathered(d):
        theirs = pl.ds(lax.rem(nar - d + N, N) * PR, PR)
        return pltpu.make_async_remote_copy(
            src_ref=out16, dst_ref=all16.at[theirs], send_sem=s4.at[d], recv_sem=r4.at[d],
            device_id={"narrow": lax.rem(nar + d, N)}, device_id_type=MESH,
        )

    def scatter_scale(d):
        return pltpu.make_async_remote_copy(
            src_ref=psc.at[d], dst_ref=rsc.at[d], send_sem=s8.at[d], recv_sem=r8.at[d],
            device_id={"narrow": lax.rem(nar + d, N)}, device_id_type=MESH,
        )

    def gather_scale(d, slot):
        return pltpu.make_async_remote_copy(
            src_ref=osc, dst_ref=asc.at[slot], send_sem=s9.at[d], recv_sem=r9.at[d],
            device_id={"narrow": lax.rem(nar + d, N)}, device_id_type=MESH,
        )

    lane8 = lax.broadcasted_iota(jnp.int32, (8, BS), 1)

    def gram_copy(d):
        return pltpu.make_async_remote_copy(
            src_ref=gs, dst_ref=gr.at[d], send_sem=s5.at[d], recv_sem=r5.at[d],
            device_id={"wide": up_peer(d)}, device_id_type=MESH,
        )

    def gram_sum(value):
        gs[:, : 2 * R] = value
        gr[0, :, : 2 * R] = value
        for d in range(1, W):
            gram_copy(d).start()
        for d in range(1, W):
            gram_copy(d).wait_recv()
        summed = jnp.zeros((2 * R, 2 * R), jnp.float32)
        for s in range(W):
            summed += gr[lax.rem(me - s + W, W)][:, : 2 * R]
        for d in range(1, W):
            gram_copy(d).wait_send()
        return summed / total

    gs[...] = jnp.zeros_like(gs)
    xs[:R, :] = q_ref[...]
    xs[R:, :] = jnp.zeros((R, B * BS), jnp.float32)
    prev[...] = jnp.zeros_like(prev)
    up[...] = jnp.zeros_like(up)
    start = gram_sum(dot_nt(xs[...], xs[...], HIGH))
    _, _, inverse0 = factor_of(start[:R, :R], R)
    xs[:R, :] = dot32(inverse0, q_ref[...])

    def step(k, carry):
        for b in range(B):
            value = xs[:R, b * BS : (b + 1) * BS]
            blocks[b] = value
            whole, unit_of = coded(value)
            coded_blocks[b] = whole
            scales[b] = jnp.broadcast_to(unit_of, (R, BS))
        for d in range(W):
            spread = jnp.zeros((R, BS), jnp.float32)
            for c in range(C):
                value = coded_blocks[local[d * C + c]]
                (rb if d == 0 else sb)[pl.ds((d * C + c) * R, R), :] = value
                spread = jnp.where(lane == c, scales[local[d * C + c]], spread)
            (rs1 if d == 0 else ss)[pl.ds(d * R, R), :] = spread
            if d:
                request(d).start()
                request_scale(d).start()

        def group(d, carry):
            @pl.when(d > 0)
            def _():
                request(d).wait_recv()
                request_scale(d).wait_recv()

            scale_rows = pl.ds(pl.multiple_of(d * R, R), R)
            scale = rs1[scale_rows, :]
            spread = jnp.zeros((R, BS), jnp.float32)
            for c in range(C):
                p = d * C + c
                rows = pl.ds(pl.multiple_of(p * R, R), R)
                tile = tiles[p]
                high, low = split(number(rb[rows, :]))
                left = jnp.concatenate(
                    [
                        jnp.concatenate([high, high], axis=1),
                        jnp.concatenate([low, jnp.zeros_like(low)], axis=1),
                    ],
                    axis=0,
                )
                both = dot_nt(left, tile)
                tf[rows, :] = (both[:R] + both[R:]) * scale[:, c : c + 1]
                high, low = split(blocks[first[p]])
                both = jnp.dot(
                    jnp.concatenate([high, low], axis=0), tile, preferred_element_type=jnp.float32
                )
                whole, unit_of = coded(both[:R, :BS] + both[R:, :BS] + both[:R, BS:])
                sb2[rows, :] = whole
                spread = jnp.where(lane == c, unit_of, spread)
            ss2[scale_rows, :] = spread

            @pl.when(d > 0)
            def _():
                answer(d).start()
                answer_scale(d).start()

            return carry

        lax.fori_loop(0, W, group, 0)
        for d in range(W):
            if d:
                answer(d).wait_recv()
                answer_scale(d).wait_recv()
            scale = (rs2 if d else ss2)[pl.ds(d * R, R), :]
            for c in range(C):
                rows = pl.ds((d * C + c) * R, R)
                rb2[rows, :] = number((rq if d else sb2)[rows, :]) * scale[:, c : c + 1]

        one_hot = owners[...]
        for n in range(1, N + 1):
            part = lax.rem(nar + n, N)
            spread = jnp.zeros((8, BS), jnp.float32)
            for q in range(RN):
                r = part * RN + q
                x = jnp.concatenate(
                    [tf[pl.ds(r, W * C, stride=R), :], rb2[pl.ds(r, W * C, stride=R), :]], axis=0
                )
                high, low = split(x)
                value = jnp.dot(
                    one_hot,
                    jnp.concatenate([high, low], axis=0),
                    preferred_element_type=jnp.float32,
                )
                if n == N:
                    acc[pl.ds(q * B, B), :] = value
                else:
                    whole, unit_of = coded(value, (0, 1))
                    pb[pl.ds(pl.multiple_of(part * PR + q * B, B), B), :] = whole
                    spread = jnp.where(lane8 == q, unit_of, spread)
            if n < N:
                psc[n] = spread
                scatter(n).start()
                scatter_scale(n).start()
        for d in range(1, N):
            scatter(d).wait_recv()
            scatter_scale(d).wait_recv()
        spread = jnp.zeros((8, BS), jnp.float32)
        for q in range(RN):
            rows = pl.ds(q * B, B)
            value = acc[rows, :]
            for d in range(1, N):
                value += number(rs[d, rows, :]) * rsc[d][:1, q : q + 1]
            whole, unit_of = coded(value, (0, 1))
            out16[rows, :] = whole
            all16[pl.ds(pl.multiple_of(nar * PR + q * B, B), B), :] = whole
            spread = jnp.where(lane8 == q, unit_of, spread)
        osc[...] = spread
        asc[nar] = spread
        for d in range(1, N):
            gather(d).start()
            gather_scale(d, nar).start()
        for d in range(1, N):
            gathered(d).wait_recv()
            gather_scale(d, lax.rem(nar - d + N, N)).wait_recv()
        for r in range(R):
            rows = pl.ds(r * B, B)
            unit_of = asc[r // RN][:1, r % RN : r % RN + 1]
            ag[rows, :] = number(all16[rows, :]) * unit_of

        for b in range(B):
            xs[R:, b * BS : (b + 1) * BS] = ag[pl.ds(b, R, stride=B), :]
        xs[R:, :] = xs[R:, :] - dot32(up[...], prev[...])
        summed = gram_sum(dot_nt(xs[...], xs[...], HIGH))
        basis_gram = summed[:R, :R]
        along = summed[:R, R:]
        along_t = summed[R:, :R]
        raw = summed[R:, R:]
        gram = raw - 2.0 * dot32(along_t, along) + dot32(along_t, dot32(basis_gram, along))
        lower, upper, inverse = factor_of(gram, R)
        coef[k, 0] = along
        coef[k, 1] = lower
        prev[...] = xs[:R, :]
        up[...] = upper
        mix = jnp.concatenate([-dot32(inverse, along_t), inverse], axis=1)
        xs[:R, :] = dot32(mix, xs[...])

        for d in range(1, W):
            request(d).wait_send()
            answer(d).wait_send()
            request_scale(d).wait_send()
            answer_scale(d).wait_send()
        for d in range(1, N):
            scatter(d).wait_send()
            gather(d).wait_send()
            scatter_scale(d).wait_send()
            gather_scale(d, nar).wait_send()
        return carry

    lax.fori_loop(0, STEPS, step, 0)
    out[...] = xs[:R, :]


def quarter_scale(code):
    return jnp.exp(code.astype(jnp.float32) * (1.0 / LOG_STEPS))


def packed(values):
    top = jnp.abs(values[0])
    for value in values[1:]:
        top = jnp.maximum(top, jnp.abs(value))
    top = jnp.maximum(jnp.max(top, axis=1, keepdims=True), 1e-30)
    whole = jnp.ceil(jnp.log(top) * LOG_STEPS).astype(jnp.int32)
    whole = jnp.broadcast_to(whole, values[0].shape)
    factor = LEVELS / quarter_scale(whole)
    out = [
        jnp.clip(jnp.round(value * factor), -LEVELS, LEVELS).astype(jnp.int32).astype(jnp.int16)
        for value in values
    ]
    return out + [whole.astype(jnp.int16)]


SLOTS = 5
Z_ROWS = 48
PARTS = 4


def fused_kernel(dims, names, points_ref, q_ref, pairs_ref, out, coef, *refs):
    W, N, C, R, B, F, total = dims
    s_ = dict(zip(names, refs))
    (points, unit, uq0, uq1, uq2, uq3, uq4, kt, tf1, tf2, vo, vr, rep, perm, shift, yt, zt, oht1, oht2, oh1, oh2, lv, ls, idx_i, idx_j, idx_v, n2, w2, o1n, o1w, i1n, i1w,
     y1, y2, gs, gn, gt, gw, qc, pv, wp, zp, at, inv, up) = (s_[n] for n in DATA)
    sem = s_
    taken = pltpu.make_async_copy(points_ref, points, sem["m_points"])
    taken.start()
    uq = (uq0, uq1, uq2, uq3, uq4)
    QR = BS // N
    JQ = B // N
    HALF = W * C
    me = lax.axis_index("wide")
    nar = lax.axis_index("narrow")
    z, x = lax.div(me, 2), lax.rem(me, 2)
    h = lax.div(z, 2)
    e = lax.rem(z, 2)
    cd = (1 - h) * (3 - z) + h * (z - 2)
    cs = (1 - h) * (z + 2) + h * (3 - z)
    ax = 1 - x
    side = z + 1 - 2 * e
    XN = 2 * z + ax
    SRC = [XN, 2 * cs + x, 2 * cs + ax, 2 * side + (1 - e) * ax + e * x]
    DST = [XN, 2 * cd + x, 2 * cd + ax, 2 * side + (1 - e) * x + e * ax]
    GROUP = [me] + SRC
    lane = lax.broadcasted_iota(jnp.int32, (R, BS), 1)
    lane8 = lax.broadcasted_iota(jnp.int32, (8, BS), 1)
    sub8 = lax.broadcasted_iota(jnp.int32, (8, BS), 0)

    def slot_is(s, lanes=None):
        lanes = lane if lanes is None else lanes
        return (lanes >= s * QR) & (lanes < s * QR + QR)

    def filled(value):
        value = value + pltpu.roll(value, QR, 1)
        return value + pltpu.roll(value, 2 * QR, 1)

    def remote(src, dst, name, at_, where):
        return pltpu.make_async_remote_copy(
            src_ref=src, dst_ref=dst, send_sem=sem["s_" + name].at[at_], recv_sem=sem["r_" + name].at[at_],
            device_id=where, device_id_type=MESH,
        )

    def wide(d):
        return {"wide": d}

    def nearby(d):
        return {"narrow": lax.rem(nar + d, N)}

    def behind(d):
        return lax.rem(nar - d + N, N)

    PART = B // PARTS

    def part(s, t):
        return uq[s].at[pl.ds(t * PART, PART)]

    def hop_x(t):
        return remote(part(0, t), part(1, t), "px", t, wide(XN))

    def hop_c(t):
        return remote(part(0, t), part(2, t), "pc", t, wide(DST[1]))

    def hop_f(t):
        return remote(part(2, t), part(3, t), "pf", t, wide(XN))

    def hop_a(t, s=0):
        return remote(part(s, t), part(4, t), "pa", t, wide(2 * side + x))

    def list_near(d):
        return remote(pairs_ref, lv.at[0, nar], "ln", d, nearby(d))

    def list_wide(d):
        return remote(lv.at[0], lv.at[d], "lw", d, wide(DST[d]))

    def vec_near(k, d):
        return remote(n2.at[k, nar], n2.at[k, nar], "vn", (k, d), nearby(d))

    def vec_near_in(k, d):
        place = n2.at[k, behind(d)]
        return remote(place, place, "vn", (k, d), nearby(d))

    def vec_wide(k, d):
        return remote(n2.at[k, nar], w2.at[k, d], "vw", (k, d), wide(DST[d]))

    def sum_near(k, d):
        return remote(o1n.at[k, d], i1n.at[k, d], "sn", (k, d), nearby(d))

    def sum_wide(k, d):
        return remote(o1w.at[k, d], i1w.at[k, d], "sw", (k, d), wide(SRC[d]))

    def gram_near(k, d):
        return remote(gs.at[k], gn.at[k, nar], "gn", (k, d), nearby(d))

    def gram_near_in(k, d):
        place = gn.at[k, behind(d)]
        return remote(place, place, "gn", (k, d), nearby(d))

    def gram_wide(k, d):
        return remote(gt.at[k], gw.at[k, me], "gw", (k, d), wide(lax.rem(me + d, W)))

    def gram_wide_in(k, d):
        place = gw.at[k, lax.rem(me - d + W, W)]
        return remote(place, place, "gw", (k, d), wide(lax.rem(me + d, W)))

    barrier = pltpu.get_barrier_semaphore()
    for d in range(1, W):
        pl.semaphore_signal(barrier, inc=1, device_id=wide(lax.rem(me + d, W)), device_id_type=MESH)
    for d in range(1, N):
        pl.semaphore_signal(barrier, inc=1, device_id=nearby(d), device_id_type=MESH)

    def normalise(b, carry):
        unit[b] = unit_rows(points[pl.ds(pl.multiple_of(b * BS, BS), BS), :])
        return carry

    def quarter(b, carry):
        uq0[b] = unit_rows(points[pl.ds(pl.multiple_of(b * BS + nar * QR, QR), QR), :])
        return carry


    def square(x_):
        four = jnp.concatenate([x_] * (BS // (2 * R)), axis=0)
        full = dot_nt(x_, four, HIGH)
        small = jnp.zeros((8, BS), jnp.float32)
        for a in range(2 * R // 8):
            small = jnp.where(slot_is(a, lane8), full[8 * a : 8 * a + 8], small)
        return small

    def gram_value(k):
        total_ = gw[k, 0]
        for d in range(1, W):
            total_ = total_ + gw[k, d]
        rows = [total_] + [pltpu.roll(total_, BS - a * 2 * R, 1) for a in range(1, 2 * R // 8)]
        return jnp.concatenate(rows, axis=0)[:, : 2 * R] / total

    def gram_send(k):
        gw[k, me] = gt[k]
        for d in range(1, W):
            gram_wide(k, d).start()

    def gram_collect(k):
        for d in range(1, N):
            gram_near_in(k, d).wait_recv()
        value = gn[k, 0]
        for d in range(1, N):
            value = value + gn[k, d]
        gt[k] = value
        gram_send(k)

    def gram_start(k):
        value = square(jnp.concatenate([qc[...], wp[...]], axis=0))
        gs[k] = value
        gn[k, nar] = value
        for d in range(1, N):
            gram_near(k, d).start()

    def gram_finish(k):
        for d in range(1, W):
            gram_wide_in(k, d).wait_recv()
        summed = gram_value(k)
        along = summed[:R, R:]
        along_t = summed[R:, :R]
        gram = summed[R:, R:] - 2.0 * dot32(along_t, along) + dot32(along_t, dot32(summed[:R, :R], along))
        lower, upper, inverse = factor_of(gram, R)
        coef[k - 1, 0] = along
        coef[k - 1, 1] = lower
        at[...] = along_t
        inv[...] = inverse
        up[...] = upper
        pv[...] = qc[...]
        qc[...] = dot32(inverse, wp[...] - dot32(along_t, qc[...]))

    lv[0, nar] = pairs_ref[...]
    q_all = q_ref[...]
    gt[0] = square(jnp.concatenate([q_all, q_all], axis=0))
    taken.wait()
    lax.fori_loop(0, B, quarter, 0, unroll=4)
    pl.semaphore_wait(barrier, W - 1 + N - 1)

    for d in range(1, N):
        list_near(d).start()
    gram_send(0)
    hop_c(0).start()
    hop_x(0).start()
    for d in range(1, N):
        place = lv.at[0, behind(d)]
        remote(place, place, "ln", d, nearby(d)).wait_recv()
    for d in range(1, 4):
        list_wide(d).start()
    for t in range(1, PARTS):
        hop_c(t).start()
        hop_x(t).start()

    @pl.when(e == 0)
    def _():
        for t in range(PARTS):
            hop_a(t).start()

    def relay_x(t):
        hop_x(t).wait_recv()

        @pl.when(e == 1)
        def _():
            hop_a(t, 1).start()

    def relay_c(t):
        hop_c(t).wait_recv()
        hop_f(t).start()

    lax.fori_loop(0, B, normalise, 0, unroll=2)

    def places(rows, columns, of):
        row = lax.broadcasted_iota(jnp.int32, (rows, columns), 0)
        column = lax.broadcasted_iota(jnp.int32, (rows, columns), 1)
        return (row == of(column)).astype(jnp.float32).astype(jnp.bfloat16)

    rep[...] = places(BS, N * BS, lambda l: (l // BS) * QR + (l & (QR - 1)))
    perm[...] = places(
        N * BS, N * BS, lambda l: ((l // QR) & (N - 1)) * BS + (l // BS) * QR + (l & (QR - 1))
    )
    for a in range(N):
        shift[a * BS : (a + 1) * BS, :] = places(
            BS, BS, lambda l: ((l // QR + N - a) & (N - 1)) * QR + (l & (QR - 1))
        )

    relay_x(0)
    for jq in range(JQ):
        value = jnp.zeros((R, BS), jnp.float32)
        for s in range(N):
            b = N * jq + s
            one = filled(jnp.where(slot_is(nar), q_ref[:, b * BS : (b + 1) * BS], 0.0))
            value = jnp.where(slot_is(s), one, value)
        wp[:, jq * BS : (jq + 1) * BS] = value

    for d in range(1, W):
        gram_wide_in(0, d).wait_recv()
    _, _, inverse0 = factor_of(gram_value(0)[:R, :R], R)
    qc[...] = dot32(inverse0, wp[...])
    for ref in (pv, zp, at, up):
        ref[...] = jnp.zeros_like(ref)
    inv[...] = (
        lax.broadcasted_iota(jnp.int32, (R, R), 0) == lax.broadcasted_iota(jnp.int32, (R, R), 1)
    ).astype(jnp.float32)

    def lanes_of(ref):
        return [ref[:, jq * BS : (jq + 1) * BS] for jq in range(JQ)]

    def vec_send(k, ref):
        for jq, value in enumerate(packed(lanes_of(ref))):
            n2[k, nar, jq * R : (jq + 1) * R, :] = value
        for d in range(1, N):
            vec_near(k, d).start()

    def vec_far(k):
        for d in range(4):
            vec_wide(k, d).start()

    vec_send(0, qc)
    relay_x(1)
    relay_c(0)
    for d in range(1, 4):
        remote(lv.at[d], lv.at[d], "lw", d, wide(DST[d])).wait_recv()
    local = pltpu.make_async_copy(lv, ls, sem["m_ls"])
    local.start()
    local.wait()

    kinds = []
    for s in range(SLOTS):
        kinds.append((s, 0))
        if s > 1:
            kinds.append((s, 1))

    for at_kind, (s, kind) in enumerate(kinds):
        other = GROUP[s]

        def indices(mq, carry):
            ch = at_kind * N + mq
            vi = jnp.zeros((8, BS), jnp.int32)
            vj = jnp.zeros((8, BS), jnp.int32)
            for c in range(C):
                if kind == 0:
                    i = lax.rem(ls[0, mq, 0, other * C + c], B)
                    j = lax.rem(ls[0, mq, 0, HALF + other * C + c], B)
                else:
                    j = lax.rem(ls[s - 1, mq, 0, me * C + c], B)
                    i = lax.rem(ls[s - 1, mq, 0, HALF + me * C + c], B)
                idx_i[ch * C + c] = i
                idx_j[ch * C + c] = j
                idx_v[ch * C + c] = s * B + j
                vi = jnp.where(sub8 == c, i, vi)
                vj = jnp.where(sub8 == c, j, vj)
            rows = pl.ds(pl.multiple_of(ch * C, C), C)
            row = (vi & (N - 1)) * JQ + vi // N
            oht1[rows, :] = (row == lane8).astype(jnp.float32)
            row = ((vj + N - (sub8 & (N - 1))) & (N - 1)) * Z_ROWS + s * JQ + vj // N
            oht2[rows, :BS] = (row == lane8).astype(jnp.float32)
            oht2[rows, BS:] = (row == lane8 + BS).astype(jnp.float32)
            return carry

        lax.fori_loop(0, N, indices, 0)

    relay_x(2)
    relay_c(1)
    turned = jnp.transpose(oht1[...])[: oh1.shape[0]].astype(jnp.bfloat16)
    oh1[...] = jnp.concatenate([turned, turned], axis=1)
    turned = jnp.transpose(oht2[...])[: oh2.shape[0]].astype(jnp.bfloat16)
    oh2[...] = jnp.concatenate([turned, turned], axis=1)

    def tiles_of(want):
        for at_kind, (s, kind) in enumerate(kinds):
            if s != want:
                continue

            def make(mq, carry):
                ch = at_kind * N + mq
                for c in range(C):
                    p = ch * C + c
                    sim = dot_nt(uq[s][idx_j[p]], unit[idx_i[p]])
                    high, low = split(jnp.exp(KERNEL_FACTOR * (sim - 1.0)))
                    rows = pl.ds(pl.multiple_of(p * QR, QR), QR)
                    kt[rows, :BS] = high
                    kt[rows, BS:] = low
                return carry

            lax.fori_loop(0, N, make, 0, unroll=2)

    tiles_of(0)
    relay_x(3)
    relay_c(2)
    tiles_of(1)
    relay_c(3)
    vec_far(0)
    tiles_of(2)
    for t in range(PARTS):
        hop_a(t).wait_recv()
    tiles_of(4)
    for t in range(PARTS):
        hop_f(t).wait_recv()
    tiles_of(3)

    chunks = len(kinds) * N

    def unpacked(ref, k, d):
        scale = quarter_scale(ref[k, d, JQ * R : (JQ + 1) * R, :].astype(jnp.int32)) * (1.0 / LEVELS)
        return [number(ref[k, d, jq * R : (jq + 1) * R, :]) * scale for jq in range(JQ)]

    def both(value):
        return jnp.concatenate(split(value), axis=0)

    def scatter(tf, one_hot, keep):
        for r in range(0, R, 2):
            columns = []
            for q in range(2):
                high, low = split(tf[pl.ds(r + q, chunks * C, stride=R), :])
                columns.append(jnp.concatenate([high, low], axis=0))
            value = jnp.dot(
                one_hot[...], jnp.concatenate(columns, axis=1), preferred_element_type=jnp.float32
            )
            keep(r, value[:, :BS])
            keep(r + 1, value[:, BS:])

    def moved(value, matrix):
        rows = value.shape[0]
        value = jnp.dot(both(value), matrix[...], preferred_element_type=jnp.float32)
        return value[:rows] + value[rows:]

    def step(k, carry):
        for d in range(1, N):
            vec_near_in(k, d).wait_recv()
        quarters = [unpacked(n2, k, q) for q in range(N)]
        pieces = [
            jnp.concatenate([both(quarters[q][jq]) for q in range(N)], axis=1) for jq in range(JQ)
        ]
        value = jnp.dot(jnp.concatenate(pieces, axis=0), perm[...], preferred_element_type=jnp.float32)
        value = value.astype(jnp.bfloat16)
        for jq in range(JQ):
            for s in range(N):
                vo[jq * N + s] = value[2 * R * jq : 2 * R * (jq + 1), s * BS : (s + 1) * BS]
        mine = unpacked(n2, k, nar)

        def keep_remote(s, values):
            value = jnp.dot(
                jnp.concatenate([both(v) for v in values], axis=0), rep[...],
                preferred_element_type=jnp.float32,
            ).astype(jnp.bfloat16)
            for jq in range(JQ):
                for b in range(N):
                    vr[s * B + jq * N + b] = value[2 * R * jq : 2 * R * (jq + 1), b * BS : (b + 1) * BS]

        keep_remote(0, mine)

        @pl.when(k > 0)
        def _():
            gram_collect(k)

        def second(ch, carry):
            left = jnp.concatenate([vo[idx_i[ch * C + c]] for c in range(C)], axis=0)
            tile = kt[pl.ds(pl.multiple_of(ch * C * QR, C * QR), C * QR), :]
            full = dot_nt(jnp.concatenate([left, left], axis=1), tile)
            for c in range(C):
                columns = slice((c // N) * BS, (c // N + 1) * BS)
                value = full[2 * R * c : 2 * R * c + R, columns] + full[2 * R * c + R : 2 * R * (c + 1), columns]
                value = jnp.where(slot_is(c % N), value, 0.0)
                tf2[pl.ds(pl.multiple_of((ch * C + c) * R, R), R), :] = value
            return carry

        lax.fori_loop(0, chunks, second, 0, unroll=8)

        def keep2(r, value):
            for a in range(N):
                zt[r * SLOTS * JQ : (r + 1) * SLOTS * JQ, a * BS : (a + 1) * BS] = (
                    value[a * Z_ROWS : a * Z_ROWS + SLOTS * JQ]
                )

        scatter(tf2, oh2, keep2)
        batch = R // 4
        for first_r in range(0, R, batch):
            value = moved(zt[first_r * SLOTS * JQ : (first_r + batch) * SLOTS * JQ, :], shift)
            for r in range(batch):
                for s in range(SLOTS):
                    place = (r * SLOTS + s) * JQ
                    y2[s, pl.ds(first_r + r, JQ, stride=R), :] = value[place : place + JQ]
        for d in range(4):
            for jq, value in enumerate(packed([y2[d + 1, jq * R : (jq + 1) * R, :] for jq in range(JQ)])):
                o1w[k, d, jq * R : (jq + 1) * R, :] = value
            sum_wide(k, d).start()

        for d in range(4):
            remote(w2.at[k, d], w2.at[k, d], "vw", (k, d), wide(DST[d])).wait_recv()
            keep_remote(d + 1, unpacked(w2, k, d))

        def first(ch, carry):
            left = []
            for c in range(C):
                value = vr[idx_v[ch * C + c]]
                value = jnp.where(slot_is(c % N, lane2), value, jnp.zeros_like(value))
                pieces = [jnp.zeros_like(value)] * (C // N)
                pieces[c // N] = value
                left.append(jnp.concatenate(pieces, axis=1))
            tile = kt[pl.ds(pl.multiple_of(ch * C * QR, C * QR), C * QR), :]
            full = jnp.dot(jnp.concatenate(left, axis=0), tile, preferred_element_type=jnp.float32)
            for c in range(C):
                high = full[2 * R * c : 2 * R * c + R]
                low = full[2 * R * c + R : 2 * R * (c + 1)]
                tf1[pl.ds(pl.multiple_of((ch * C + c) * R, R), R), :] = (
                    high[:, :BS] + high[:, BS:] + low[:, :BS]
                )
            return carry

        lax.fori_loop(0, chunks, first, 0, unroll=8)

        def keep1(r, value):
            for s in range(N):
                yt[r * JQ : (r + 1) * JQ, s * BS : (s + 1) * BS] = value[s * JQ : (s + 1) * JQ]

        scatter(tf1, oh1, keep1)
        value = moved(yt[...], perm)
        for r in range(R):
            for q in range(N):
                y1[q, pl.ds(r, JQ, stride=R), :] = value[r * JQ : (r + 1) * JQ, q * BS : (q + 1) * BS]

        for d in range(1, N):
            to = lax.rem(nar + d, N)
            for jq, value in enumerate(packed([y1[to, jq * R : (jq + 1) * R, :] for jq in range(JQ)])):
                o1n[k, d, jq * R : (jq + 1) * R, :] = value
            sum_near(k, d).start()

        @pl.when(k > 0)
        def _():
            gram_finish(k)

        image = [y1[nar, jq * R : (jq + 1) * R, :] + y2[0, jq * R : (jq + 1) * R, :] for jq in range(JQ)]
        for d in range(4):
            sum_wide(k, d).wait_recv()
            image = [a + b for a, b in zip(image, unpacked(i1w, k, d))]
        for d in range(1, N):
            sum_near(k, d).wait_recv()
            image = [a + b for a, b in zip(image, unpacked(i1n, k, d))]
        image = jnp.concatenate(image, axis=1)
        image = dot32(inv[...], image - dot32(at[...], zp[...]))
        zp[...] = image
        wp[...] = image - dot32(up[...], pv[...])

        @pl.when(k < STEPS - 1)
        def _():
            vec_send(k + 1, wp)
            vec_far(k + 1)

        gram_start(k + 1)
        return carry

    lane2 = lax.broadcasted_iota(jnp.int32, (2 * R, BS), 1)
    lax.fori_loop(0, STEPS, step, 0)
    gram_collect(STEPS)
    gram_finish(STEPS)
    for jq, value in enumerate(packed(lanes_of(qc))):
        n2[STEPS, nar, jq * R : (jq + 1) * R, :] = value
    for d in range(1, N):
        vec_near(STEPS, d).start()
    for d in range(1, N):
        vec_near_in(STEPS, d).wait_recv()
    pieces = [jnp.concatenate(unpacked(n2, STEPS, q), axis=0) for q in range(N)]
    value = moved(jnp.concatenate(pieces, axis=1), perm)
    for jq in range(JQ):
        for s in range(N):
            b = jq * N + s
            out[:, b * BS : (b + 1) * BS] = value[jq * R : (jq + 1) * R, s * BS : (s + 1) * BS]

    for t in range(PARTS):
        hop_x(t).wait_send()
        hop_c(t).wait_send()
        hop_a(t).wait_send()
        hop_f(t).wait_send()
    for d in range(1, N):
        list_near(d).wait_send()
        vec_near(STEPS, d).wait_send()
    for d in range(1, 4):
        list_wide(d).wait_send()
    for d in range(1, W):
        gram_wide(0, d).wait_send()
    for k in range(STEPS):
        for d in range(1, N):
            vec_near(k, d).wait_send()
            sum_near(k, d).wait_send()
            gram_near(k + 1, d).wait_send()
        for d in range(4):
            vec_wide(k, d).wait_send()
            sum_wide(k, d).wait_send()
        for d in range(1, W):
            gram_wide(k + 1, d).wait_send()


DATA = (
    "points", "unit", "uq0", "uq1", "uq2", "uq3", "uq4", "kt", "tf1", "tf2", "vo", "vr", "rep", "perm", "shift", "yt", "zt", "oht1", "oht2",
    "oh1", "oh2", "lv", "ls", "idx_i", "idx_j", "idx_v", "n2", "w2", "o1n", "o1w", "i1n", "i1w", "y1", "y2",
    "gs", "gn", "gt", "gw", "qc", "pv", "wp", "zp", "at", "inv", "up",
)


def fused(points, q_init, pairs, W, N):
    R, cols = q_init.shape
    F = points.shape[1]
    B = cols // BS
    pair_count = pairs.shape[1]
    C = pair_count // W
    QR, JQ = BS // N, B // N
    P_ = (SLOTS + SLOTS - 2) * N * C
    f32, bf16, i16, i32 = jnp.float32, jnp.bfloat16, jnp.int16, jnp.int32
    V = pltpu.VMEM
    message = ((JQ + 1) * R, BS)
    rounds = STEPS + 1
    columns = JQ * BS
    shapes = {
        "points": V(points.shape, bf16), "unit": V((B, BS, F), bf16), **{f"uq{s}": V((B, QR, F), bf16) for s in range(SLOTS)}, "kt": V((P_ * QR, 2 * BS), bf16),
        "tf1": V((P_ * R, BS), f32), "tf2": V((P_ * R, BS), f32),
        "vo": V((B, 2 * R, BS), bf16), "vr": V((SLOTS * B, 2 * R, BS), bf16),
        "oht1": V((P_, BS), f32), "oht2": V((P_, 2 * BS), f32),
        "rep": V((BS, N * BS), bf16), "perm": V((N * BS, N * BS), bf16), "shift": V((N * BS, BS), bf16),
        "yt": V((R * JQ, N * BS), f32), "zt": V((R * SLOTS * JQ, N * BS), f32),
        "oh1": V((B, 2 * P_), bf16), "oh2": V((N * Z_ROWS, 2 * P_), bf16),
        "lv": V((4, N, 1, 2 * pair_count), i32), "ls": pltpu.SMEM((4, N, 1, 2 * pair_count), i32),
        "idx_i": pltpu.SMEM((P_,), i32), "idx_j": pltpu.SMEM((P_,), i32),
        "idx_v": pltpu.SMEM((P_,), i32),
        "n2": V((rounds, N) + message, i16), "w2": V((STEPS, 4) + message, i16),
        "o1n": V((STEPS, N) + message, i16), "o1w": V((STEPS, 4) + message, i16),
        "i1n": V((STEPS, N) + message, i16), "i1w": V((STEPS, 4) + message, i16),
        "y1": V((N, JQ * R, BS), f32), "y2": V((SLOTS, JQ * R, BS), f32),
        "gs": V((rounds, 8, BS), f32), "gn": V((rounds, N, 8, BS), f32),
        "gt": V((rounds, 8, BS), f32), "gw": V((rounds, W, 8, BS), f32),
        "qc": V((R, columns), f32), "pv": V((R, columns), f32), "wp": V((R, columns), f32),
        "zp": V((R, columns), f32),
        "at": V((R, R), f32), "inv": V((R, R), f32), "up": V((R, R), f32),
    }
    sems = {
        "px": (PARTS,), "pc": (PARTS,), "pf": (PARTS,), "pa": (PARTS,), "ln": (N,), "lw": (4,),
        "vn": (rounds, N), "vw": (STEPS, 4), "sn": (STEPS, N), "sw": (STEPS, 4),
        "gn": (rounds, N), "gw": (rounds, W),
    }
    names = list(DATA)
    scratch = [shapes[n] for n in DATA]
    for name, shape in sems.items():
        for way in "sr":
            names.append(way + "_" + name)
            scratch.append(pltpu.SemaphoreType.DMA(shape))
    for name in ("m_ls", "m_points"):
        names.append(name)
        scratch.append(pltpu.SemaphoreType.DMA)
    vmem = pl.BlockSpec(memory_space=pltpu.VMEM)
    dims = (W, N, C, R, B, F, B * BS * W)
    return pl.pallas_call(
        functools.partial(fused_kernel, dims, tuple(names)),
        out_shape=(
            jax.ShapeDtypeStruct((R, cols), f32),
            jax.ShapeDtypeStruct((STEPS, 2, R, R), f32),
        ),
        in_specs=[pl.BlockSpec(memory_space=pl.ANY), vmem, vmem],
        out_specs=(vmem, vmem),
        scratch_shapes=scratch,
        compiler_params=pltpu.CompilerParams(collective_id=1, has_side_effects=True),
        name="fused",
    )(points, q_init, pairs.reshape(1, 2 * pair_count))


def lanczos(first, local, owners, tiles, q_init, wide_count, narrow_count, total):
    R, cols = q_init.shape
    B = cols // BS
    pair_count = first.shape[0]
    C = pair_count // wide_count
    dims = (wide_count, narrow_count, C, R, B, total)
    vmem = pl.BlockSpec(memory_space=pltpu.VMEM)
    smem = pl.BlockSpec(memory_space=pltpu.SMEM)
    f32 = jnp.float32
    pairs_buf = pltpu.VMEM((pair_count * R, BS), f32)
    coded_buf = pltpu.VMEM((pair_count * R, BS), jnp.int16)
    scale_buf = pltpu.VMEM((wide_count * R, BS), f32)
    part = R // narrow_count * B
    wide_sem = pltpu.SemaphoreType.DMA((wide_count,))
    narrow_sem = pltpu.SemaphoreType.DMA((narrow_count,))
    return pl.pallas_call(
        functools.partial(main_kernel, dims),
        out_shape=(
            jax.ShapeDtypeStruct((R, cols), f32),
            jax.ShapeDtypeStruct((STEPS, 2, R, R), f32),
        ),
        in_specs=[smem, smem, vmem, vmem, vmem],
        out_specs=(vmem, vmem),
        scratch_shapes=[
            coded_buf, coded_buf, coded_buf, coded_buf,
            scale_buf, scale_buf, scale_buf, scale_buf,
            pltpu.VMEM((B, R, BS), jnp.int16),
            pltpu.VMEM((B, R, BS), f32),
            pairs_buf, pairs_buf,
            pltpu.VMEM((R * B, BS), jnp.int16),
            pltpu.VMEM((narrow_count, part, BS), jnp.int16),
            pltpu.VMEM((R * B, BS), f32),
            pltpu.VMEM((part, BS), f32),
            pltpu.VMEM((part, BS), jnp.int16),
            pltpu.VMEM((R * B, BS), jnp.int16),
            pltpu.VMEM((narrow_count, 8, BS), f32),
            pltpu.VMEM((narrow_count, 8, BS), f32),
            pltpu.VMEM((8, BS), f32),
            pltpu.VMEM((narrow_count, 8, BS), f32),
            pltpu.VMEM((2 * R, cols), f32),
            pltpu.VMEM((B, R, BS), f32),
            pltpu.VMEM((R, cols), f32),
            pltpu.VMEM((R, R), f32),
            pltpu.VMEM((2 * R, BS), f32),
            pltpu.VMEM((wide_count, 2 * R, BS), f32),
            wide_sem, wide_sem, wide_sem, wide_sem,
            narrow_sem, narrow_sem, narrow_sem, narrow_sem,
            wide_sem, wide_sem, wide_sem, wide_sem, wide_sem, wide_sem,
            narrow_sem, narrow_sem, narrow_sem, narrow_sem,
        ],
        compiler_params=pltpu.CompilerParams(collective_id=0, has_side_effects=True),
        name="lanczos",
    )(first, local, owners, tiles, q_init)


def per_device(points, q_init, pairs):
    wide_count = lax.axis_size("wide")
    narrow_count = lax.axis_size("narrow")
    me = lax.axis_index("wide")
    own_blocks = points.shape[0] // BS
    width = points.shape[1]
    pair_count = pairs.shape[1]
    capacity = pair_count // wide_count
    if wide_count == 8 and narrow_count == 4 and own_blocks == 8 * narrow_count and capacity == 8:
        return fused(points, q_init, pairs, wide_count, narrow_count)
    total = own_blocks * BS * wide_count
    unit = unit_rows(points).reshape(own_blocks, BS, width)
    turn = jnp.arange(wide_count, dtype=jnp.int32)
    first_rows = (pairs[0] - me * own_blocks).reshape(wide_count, capacity)
    first = first_rows[(me - turn) % wide_count].reshape(pair_count)
    second = (pairs[1].reshape(wide_count, capacity) - turn[:, None] * own_blocks)
    every = lax.all_to_all(
        jnp.broadcast_to(second.reshape(1, pair_count), (wide_count, pair_count)),
        "wide", split_axis=0, concat_axis=0, tiled=True,
    ).reshape(wide_count, wide_count, capacity)
    local_ids = lax.dynamic_index_in_dim(every, me, axis=1, keepdims=False)
    local = local_ids[(me + turn) % wide_count].reshape(pair_count)
    targets = jnp.concatenate([first, local, first, local])
    owners = (jnp.arange(own_blocks, dtype=jnp.int32)[:, None] == targets[None, :]).astype(
        jnp.bfloat16
    )
    blocks = lax.all_to_all(
        unit[local_ids.reshape(pair_count)], "wide", split_axis=0, concat_axis=0, tiled=True
    ).reshape(wide_count, capacity, BS, width)
    tiles = make_tiles(jnp.reshape(me, (1,)).astype(jnp.int32), first, unit, blocks)
    return lanczos(first, local, owners, tiles, q_init, wide_count, narrow_count, total)


def solution(mesh):
    placed = (P("wide", None), P(None, "wide"), P(None, ("wide", "narrow")))
    return jax.shard_map(
        per_device, mesh=mesh, in_specs=placed, out_specs=(P(None, "wide"), P()), check_vma=False
    )
```
